32 devices in a mesh: seq: 8 (over y, x, core), ch: 4 (over z).
Axes of the slice: x: 2, y: 2, z: 4, core: 2. Of those that a mesh axis runs over, the one named last changes fastest.
Arguments:
- signal: bfloat16 [1024, 128, 1024], P('seq', 'ch'), may hold values from -6 to 6
- cotangent: bfloat16 [1024, 128, 1024], P('seq', 'ch'), may hold values from -6 to 6
- right_factor: bfloat16 [1024, 1024], replicated, may hold values from -0.1875 to 0.1875
- left_factor: bfloat16 [1024, 1024], replicated, may hold values from -0.1875 to 0.1875
- right_blocks: int32 [8, 8], replicated, may hold values 0 or 1
- left_blocks: int32 [8, 8], replicated, may hold values 0 or 1
Outputs:
- mixed: bfloat16 [1024, 128, 1024], P('seq', 'ch')
- grad_signal: bfloat16 [1024, 128, 1024], P('seq', 'ch')
- grad_right: float32 [1024, 1024], P('seq', 'ch')
- grad_left: float32 [1024, 1024], P('seq', 'ch')
The draws below stay inside these ranges and needn't reach their ends.
All inputs are finite; a program needn't handle non-finite values.
Results may differ from the reference program's by a relative error of at most 0.0051.
Values may be sent and summed in bfloat16 or wider, within the bound.
A program may use at most 192 MiB of HBM per device.

```python
import math
import jax
import jax.numpy as jnp
from jax import lax

M1 = 1024
M2 = 1024
C = 128
MB1 = 8
MB2 = 8


def touch_ends(values, own_key, low, high):
    spot = [jax.random.randint(jax.random.fold_in(own_key, axis), (), 0, length) for axis, length in enumerate(values.shape)]
    widest = values.shape.index(max(values.shape))
    beside = spot[:widest] + [(spot[widest] + 1) % values.shape[widest]] + spot[widest + 1:]
    return values.at[tuple(spot)].set(low).at[tuple(beside)].set(high)


def levels(own_key, extent, cuts, least, top_value):
    gain, own = 1.0, jax.random.fold_in(own_key, 6)
    for dim, blocks in cuts:
        draws = jnp.exp(jax.random.uniform(jax.random.fold_in(own, dim), (blocks,), jnp.float32, least / len(cuts), top_value / len(cuts)))
        gain = gain * jnp.repeat(draws, extent[dim] // blocks).reshape([-1 if axis == dim else 1 for axis in range(len(extent))])
    return gain


def noise(rng, extent, spread, most, cuts=(), held_as=jnp.bfloat16):
    level = levels(rng, extent, cuts, -0.22, 0.18) if cuts else 1.0
    drawn = jax.random.normal(rng, extent, jnp.float32) * spread * level
    return jnp.minimum(jnp.maximum(drawn, -most), most).astype(held_as)


def setup_inputs(seed: int = 0) -> dict:
    arg_keys = jax.random.split(jax.random.key(seed), 7)
    return {
        "signal": noise(arg_keys[0], (M1, C, M2), 1.0, 6.0, ((0, 8), (1, 4))),
        "cotangent": noise(arg_keys[1], (M1, C, M2), 1.0, 6.0, ((0, 8), (1, 4))),
        "right_factor": noise(arg_keys[2], (M2, M2), M2 ** -0.5, 0.1875),
        "left_factor": noise(arg_keys[3], (M1, M1), M1 ** -0.5, 0.1875),
        "right_blocks": touch_ends((jax.random.randint(arg_keys[4], (MB2, MB2), 0, 8) < 5).astype(jnp.int32), jax.random.fold_in(arg_keys[4], 1), 0, 1),
        "left_blocks": touch_ends((jax.random.randint(arg_keys[5], (MB1, MB1), 0, 8) < 5).astype(jnp.int32), jax.random.fold_in(arg_keys[5], 1), 0, 1),
    }


def expand(blocks, width):
    tile = width // blocks.shape[0]
    return jnp.repeat(jnp.repeat(blocks, tile, axis=0), tile, axis=1)

def reference(signal, cotangent, right_factor, left_factor, right_blocks, left_blocks):
    right_mask = expand(right_blocks, M2).astype(jnp.bfloat16)
    left_mask = expand(left_blocks, M1).astype(jnp.bfloat16)
    right_eff = right_factor * right_mask
    left_eff = left_factor * left_mask
    block = math.gcd(C, 8)
    groups = C // block

    def split(array):
        return array.reshape(M1, groups, block, M2).transpose(1, 0, 2, 3)

    def step(carry, pieces):
        sig, cot = pieces
        flat = sig.reshape(M1 * block, M2)
        z_rows = jnp.dot(flat, right_eff.T, preferred_element_type=jnp.float32).astype(jnp.bfloat16)
        z_cols = z_rows.reshape(M1, block * M2)
        y_val = jnp.dot(left_eff, z_cols, preferred_element_type=jnp.float32).astype(jnp.bfloat16)
        y_val = y_val.reshape(M1, block, M2).astype(jnp.float32)
        sig_f = sig.astype(jnp.float32)
        gate = jax.nn.sigmoid(sig_f)
        swish = sig_f * gate
        mixed = (sig_f + y_val * swish).astype(jnp.bfloat16)
        cot_f = cot.astype(jnp.float32)
        grad_y = (cot_f * swish).astype(jnp.bfloat16)
        grad_cols = grad_y.reshape(M1, block * M2)
        grad_z = jnp.dot(left_eff.T, grad_cols, preferred_element_type=jnp.float32).astype(jnp.bfloat16)
        grad_flat = grad_z.reshape(M1 * block, M2)
        left_term = jnp.dot(grad_cols, z_cols.T, preferred_element_type=jnp.float32)
        right_term = jnp.dot(grad_flat.T, flat, preferred_element_type=jnp.float32)
        back = jnp.dot(grad_flat, right_eff, preferred_element_type=jnp.float32).reshape(M1, block, M2)
        dswish = gate * (1.0 + sig_f * (1.0 - gate))
        grad_sig = (cot_f * (1.0 + y_val * dswish) + back).astype(jnp.bfloat16)
        return ((carry[0] + right_term, carry[1] + left_term), (mixed, grad_sig))
    init = (jnp.zeros((M2, M2), jnp.float32), jnp.zeros((M1, M1), jnp.float32))
    sums, stacked = lax.scan(step, init, (split(signal), split(cotangent)))

    def merge(array):
        return array.transpose(1, 0, 2, 3).reshape(M1, C, M2)
    grad_right = sums[0] * right_mask.astype(jnp.float32) / math.sqrt(M1 * C)
    grad_left = sums[1] * left_mask.astype(jnp.float32) / math.sqrt(M2 * C)
    return (merge(stacked[0]), merge(stacked[1]), grad_right, grad_left)
```

```python
import functools
import math

import jax
import jax.numpy as jnp
from jax import lax
from jax.experimental import pallas as pl
from jax.experimental.pallas import tpu as pltpu
from jax.sharding import PartitionSpec as P


def expand(blocks, width):
    tile = width // blocks.shape[0]
    return jnp.repeat(jnp.repeat(blocks, tile, axis=0), tile, axis=1)


def to_columns(rows, peers):
    rows_here, chans, width_two = rows.shape
    piece = width_two // peers
    arranged = rows.reshape(rows_here, chans, peers, piece).transpose(0, 2, 1, 3)
    return arranged.reshape(rows_here, peers, chans * piece)


def to_rows(received, chans):
    rows_here, peers, wide = received.shape
    piece = wide // chans
    arranged = received.reshape(rows_here, peers, chans, piece).transpose(0, 2, 1, 3)
    return arranged.reshape(rows_here, chans, peers * piece)


def shards_by_column(signal, cotangent, right_factor, left_factor, right_blocks, left_blocks):
    rows_here, chans, width_two = signal.shape
    width_one = left_factor.shape[0]
    peers = lax.axis_size("seq")
    right_mask = expand(right_blocks, width_two).astype(jnp.bfloat16)
    left_mask = expand(left_blocks, width_one).astype(jnp.bfloat16)
    right_eff = right_factor * right_mask
    left_eff = left_factor * left_mask
    flat_signal = signal.reshape(rows_here * chans, width_two)
    first_rows = jnp.dot(flat_signal, right_eff.T, preferred_element_type=jnp.float32)
    first_rows = to_columns(
        first_rows.astype(jnp.bfloat16).reshape(rows_here, chans, width_two), peers
    )
    sig_f = signal.astype(jnp.float32)
    gate = jax.nn.sigmoid(sig_f)
    swish = sig_f * gate
    cot_f = cotangent.astype(jnp.float32)
    grad_rows = to_columns((cot_f * swish).astype(jnp.bfloat16), peers)
    z_cols = lax.all_to_all(first_rows, "seq", split_axis=1, concat_axis=0, tiled=True)
    flat_cols = z_cols.reshape(width_one, z_cols.shape[2])
    result = jnp.dot(left_eff, flat_cols, preferred_element_type=jnp.float32)
    y_cols = result.astype(jnp.bfloat16).reshape(width_one, 1, z_cols.shape[2])
    y_back = lax.all_to_all(y_cols, "seq", split_axis=0, concat_axis=1, tiled=True)
    dy_cols = lax.all_to_all(grad_rows, "seq", split_axis=1, concat_axis=0, tiled=True)
    flat_cols = dy_cols.reshape(width_one, dy_cols.shape[2])
    result = lax.dot_general(
        left_eff, flat_cols, (((0,), (0,)), ((), ())), preferred_element_type=jnp.float32
    )
    dz_cols = result.astype(jnp.bfloat16).reshape(width_one, 1, dy_cols.shape[2])
    dz_back = lax.all_to_all(dz_cols, "seq", split_axis=0, concat_axis=1, tiled=True)
    y_rows = to_rows(y_back, chans)
    dz_rows = to_rows(dz_back, chans)
    y_f = y_rows.astype(jnp.float32)
    mixed = (sig_f + y_f * swish).astype(jnp.bfloat16)
    dz_flat = dz_rows.reshape(rows_here * chans, width_two)
    back = jnp.dot(dz_flat, right_eff, preferred_element_type=jnp.float32).reshape(
        rows_here, chans, width_two
    )
    dswish = gate * (1.0 + sig_f * (1.0 - gate))
    grad_signal = (cot_f * (1.0 + y_f * dswish) + back).astype(jnp.bfloat16)
    wide = z_cols.shape[2]
    z_flat = z_cols.reshape(width_one, wide)
    dy_flat = dy_cols.reshape(width_one, wide)
    left_term = lax.dot_general(
        dy_flat, z_flat, (((1,), (1,)), ((), ())), preferred_element_type=jnp.float32
    )
    right_term = lax.dot_general(
        dz_flat, flat_signal, (((0,), (0,)), ((), ())), preferred_element_type=jnp.float32
    )
    total_chans = chans * lax.axis_size("ch")
    right_term = right_term * right_mask.astype(jnp.float32) / math.sqrt(width_one * total_chans)
    left_term = left_term * left_mask.astype(jnp.float32) / math.sqrt(width_two * total_chans)
    partial_value = (
        lax.psum_scatter(right_term, "seq", scatter_dimension=0, tiled=True),
        lax.psum_scatter(left_term, "seq", scatter_dimension=0, tiled=True),
    )
    grad_right, grad_left = (
        lax.psum_scatter(partial_value[0], "ch", scatter_dimension=1, tiled=True),
        lax.psum_scatter(partial_value[1], "ch", scatter_dimension=1, tiled=True),
    )
    return (mixed, grad_signal, grad_right, grad_left)


def mix_kernel(
    peers, groups, parts, chunks, scales, right_blocks, left_blocks, signal, cotangent, right_in, left_in,
    out_m, out_g, out_r, out_l, xh, ch, mt, gt,
    right, left, grad_r, grad_l, xbuf, cbuf, zbuf, dybuf, dzbuf, pairs, along, summed, across, slab, facing, turned,
    send_sem, recv_sem, own_in_sem, stage_sem, last_send, last_recv, pair_sems, along_sems, across_sems, load_sem,
):
    me = lax.axis_index("seq")
    column = lax.axis_index("ch")
    rows = signal.shape[0]
    width = signal.shape[2]
    order = left.shape[0]
    tile = 256
    piece = rows // chunks
    last = parts - 1

    def own_rows(who):
        return pl.ds(pl.multiple_of(who * rows, rows), rows)

    def some_rows(who, chunk):
        return pl.ds(pl.multiple_of(who * rows + chunk * piece, piece), piece)

    def remote(source, target, going, coming, who):
        return pltpu.make_async_remote_copy(
            src_ref=source,
            dst_ref=target,
            send_sem=going,
            recv_sem=coming,
            device_id=(who, column),
            device_id_type=pl.DeviceIdType.MESH,
        )

    def each_peer(action):
        @pl.loop(1, peers)
        def _(step):
            action(lax.rem(me + step, peers))

    barrier = pltpu.get_barrier_semaphore()

    def load(part, kind, source):
        there = pl.ds(pl.multiple_of(part * peers, peers), peers)
        return pltpu.make_async_copy(source.at[:, there, :], slab, load_sem.at[kind])

    load(0, 0, signal).start()

    def greet(who):
        pl.semaphore_signal(
            barrier, inc=1, device_id=(who, column), device_id_type=pl.DeviceIdType.MESH
        )

    each_peer(greet)

    @pl.loop(1, groups)
    def _(step):
        pl.semaphore_signal(
            barrier,
            inc=1,
            device_id=(me, lax.rem(column + step, groups)),
            device_id_type=pl.DeviceIdType.MESH,
        )

    inputs = ((0, signal, xh), (1, cotangent, ch))
    outputs = ((2, mt, xh, xbuf, out_m), (3, gt, ch, cbuf, out_g))

    def turn(part, kind, chunk, count):
        @pl.loop(chunk * (piece // 16), (chunk + count) * (piece // 16))
        def _(step):
            here = pl.ds(pl.multiple_of(step * 16, 16), 16)
            turned[lax.rem(part, 2), kind, :, here, :] = jnp.swapaxes(slab[here], 0, 1)

    def in_copy(kind, part, held, who, at_rows, there):
        return remote(
            turned.at[lax.rem(part, 2), kind, who, at_rows],
            held.at[part, there],
            send_sem.at[kind, part, who],
            recv_sem.at[kind, part, me],
            who,
        )

    def whole_in_copy(kind, part, held, who):
        return in_copy(kind, part, held, who, pl.ds(0, rows), own_rows(me))

    def own_copy(kind, part, held):
        return pltpu.make_async_copy(
            turned.at[lax.rem(part, 2), kind, me], held.at[part, own_rows(me)], own_in_sem.at[kind, part]
        )

    def send_in(part):
        for kind, source, held in inputs:
            load(part, kind, source).wait()
            turn(part, kind, 0, chunks)
            if kind == 0:
                load(part, 1, cotangent).start()
            each_peer(lambda who: whole_in_copy(kind, part, held, who).start())
            own_copy(kind, part, held).start()

    def send_first():
        for kind, source, held in inputs:
            load(0, kind, source).wait()
            for chunk in range(chunks):
                turn(0, kind, chunk, 1)
                if kind == 0 and chunk == 0:
                    pl.semaphore_wait(barrier, peers - 1 + groups - 1)
                each_peer(
                    lambda who: in_copy(
                        kind, 0, held, who, pl.ds(chunk * piece, piece), some_rows(me, chunk)
                    ).start()
                )
            if kind == 0:
                load(0, 1, cotangent).start()
            own_copy(kind, 0, held).start()

    def wait_in(part):
        def one(who):
            for kind, source, held in inputs:
                remote(
                    turned.at[lax.rem(part, 2), kind, who], held.at[part, own_rows(who)],
                    send_sem.at[kind, part, who], recv_sem.at[kind, part, who], who,
                ).wait_recv()

        each_peer(one)
        for kind, source, held in inputs:
            own_copy(kind, part, held).wait()

    def wait_in_sent(part):
        def one(who):
            for kind, source, held in inputs:
                whole_in_copy(kind, part, held, who).wait_send()

        each_peer(one)

    def fetch(part):
        copies = [
            pltpu.make_async_copy(held.at[part], buf, stage_sem.at[kind - 2])
            for kind, landed, held, buf, out in outputs
        ]
        for copy in copies:
            copy.start()
        for copy in copies:
            copy.wait()

    def store(part):
        copies = []
        for kind, landed, held, buf, out in outputs:
            copies.append(pltpu.make_async_copy(buf, held.at[part], stage_sem.at[kind - 2]))
            copies.append(
                pltpu.make_async_copy(buf.at[own_rows(me)], landed.at[part * peers + me], stage_sem.at[kind])
            )
        for copy in copies:
            copy.start()
        for copy in copies:
            copy.wait()

    def out_copy(kind, part, held, landed, who, slot, sender):
        return remote(
            held.at[part, own_rows(who)], landed.at[part * peers + slot],
            send_sem.at[kind, part, who], recv_sem.at[kind, part, sender], who,
        )

    def send_out(part):
        def one(who):
            for kind, landed, held, buf, out in outputs:
                out_copy(kind, part, held, landed, who, me, me).start()

        each_peer(one)

    def last_copy(kind, chunk, held, landed, who, slot):
        return remote(
            held.at[last, some_rows(who, chunk)], landed.at[last * peers + slot, pl.ds(chunk * piece, piece)],
            last_send.at[kind - 2, chunk, who], last_recv.at[kind - 2, chunk, slot], who,
        )

    def send_last():
        for chunk in range(chunks):
            for kind, landed, held, buf, out in outputs:
                each_peer(lambda who: last_copy(kind, chunk, held, landed, who, me).start())

    def face(landed, out, part, start, count):
        copy = pltpu.make_async_copy(
            landed.at[pl.ds(part * peers, peers), pl.ds(start, count)],
            facing.at[:, pl.ds(start, count)],
            stage_sem.at[0],
        )
        copy.start()
        copy.wait()

        @pl.loop(start // 16, (start + count) // 16)
        def _(step):
            here = pl.ds(pl.multiple_of(step * 16, 16), 16)
            out[here, part * peers:(part + 1) * peers, :] = jnp.swapaxes(facing[:, here, :], 0, 1)

    def turn_out(part):
        for kind, landed, held, buf, out in outputs:
            each_peer(lambda who: out_copy(kind, part, held, landed, who, who, who).wait_recv())
            face(landed, out, part, 0, rows)

    def turn_last():
        for chunk in range(chunks):
            for kind, landed, held, buf, out in outputs:
                each_peer(lambda who: last_copy(kind, chunk, held, landed, who, who).wait_recv())
                face(landed, out, last, chunk * piece, piece)

    def wait_out_sent():
        @pl.loop(0, last)
        def _(part):
            for kind, landed, held, buf, out in outputs:
                each_peer(lambda who: out_copy(kind, part, held, landed, who, me, me).wait_send())

        for chunk in range(chunks):
            for kind, landed, held, buf, out in outputs:
                each_peer(lambda who: last_copy(kind, chunk, held, landed, who, me).wait_send())

    def at(step):
        return pl.ds(pl.multiple_of(step * tile, tile), tile)

    def dot(a, b, dims):
        return lax.dot_general(a, b, (dims, ((), ())), preferred_element_type=jnp.float32)

    def compute():
        @pl.loop(0, order // tile)
        def _(step):
            x = xbuf[at(step), :]
            zbuf[at(step), :] = dot(x, right[...], ((1,), (1,))).astype(jnp.bfloat16)
            sig = x.astype(jnp.float32)
            swish = sig * jax.nn.sigmoid(sig)
            cot = cbuf[at(step), :].astype(jnp.float32)
            dybuf[at(step), :] = (cot * swish).astype(jnp.bfloat16)

        @pl.loop(0, order // tile)
        def _(step):
            dzbuf[at(step), :] = dot(left[:, at(step)], dybuf[...], ((0,), (0,))).astype(jnp.bfloat16)
            grad_l[at(step), :] += dot(dybuf[at(step), :], zbuf[...], ((1,), (1,)))

        @pl.loop(0, width // tile)
        def _(step):
            grad_r[at(step), :] += dot(dzbuf[:, at(step)], xbuf[...], ((0,), (0,)))

        @pl.loop(0, order // tile)
        def _(step):
            y = dot(left[at(step), :], zbuf[...], ((1,), (0,))).astype(jnp.bfloat16).astype(jnp.float32)
            back = dot(dzbuf[at(step), :], right[...], ((1,), (0,)))
            sig = xbuf[at(step), :].astype(jnp.float32)
            cot = cbuf[at(step), :].astype(jnp.float32)
            gate = jax.nn.sigmoid(sig)
            xbuf[at(step), :] = (sig + y * (sig * gate)).astype(jnp.bfloat16)
            dswish = gate * (1.0 + sig * (1.0 - gate))
            cbuf[at(step), :] = (cot * (1.0 + y * dswish) + back).astype(jnp.bfloat16)

    def apply_mask(blocks, target):
        side = target.shape[0] // blocks.shape[0]

        @pl.loop(0, blocks.shape[0])
        def _(down):
            here = pl.ds(pl.multiple_of(down * side, side), side)
            for right_of in range(blocks.shape[1]):
                there = slice(right_of * side, (right_of + 1) * side)
                keep = blocks[down, right_of].astype(jnp.float32)
                target[here, there] = (target[here, there].astype(jnp.float32) * keep).astype(jnp.bfloat16)

    half = peers // 2
    parity = lax.rem(me, 2)
    chip = me // 2
    sibling = me + 1 - 2 * parity
    cols = width // groups
    grads = ((0, grad_r), (1, grad_l))

    def pair_copy(kind, grad, block):
        return remote(
            grad.at[own_rows(2 * block + 1 - parity)], pairs.at[kind, block],
            pair_sems.at[0, kind, block], pair_sems.at[1, kind, block], sibling,
        )

    def own_cols(line):
        return pl.ds(pl.multiple_of(line * cols, cols), cols)

    def along_copy(kind, other, slot, block):
        return pltpu.make_async_remote_copy(
            src_ref=zbuf.at[own_rows(kind * half + block), own_cols(other)],
            dst_ref=along.at[kind, slot, own_rows(block)],
            send_sem=along_sems.at[0, kind, other, block],
            recv_sem=along_sems.at[1, kind, slot, block],
            device_id=(me, other),
            device_id_type=pl.DeviceIdType.MESH,
        )

    def across_copy(kind, other, slot):
        return remote(
            summed.at[kind, other], across.at[kind, slot],
            across_sems.at[0, kind, other], across_sems.at[1, kind, slot], 2 * other + parity,
        )

    def start_pairs():
        @pl.loop(0, half)
        def _(block):
            for kind, grad in grads:
                pair_copy(kind, grad, block).start()

    def send_along():
        @pl.loop(0, half)
        def _(block):
            for kind, grad in grads:
                pair_copy(kind, grad, block).wait_recv()
                total = grad[own_rows(2 * block + parity), :] + pairs[kind, block]
                grad[own_rows(2 * block + parity), :] = total
                zbuf[own_rows(kind * half + block), :] = total.astype(jnp.bfloat16)

                @pl.loop(1, groups)
                def _(step):
                    along_copy(kind, lax.rem(column + step, groups), column, block).start()

    def send_across():
        @pl.loop(0, half)
        def _(block):
            for kind, grad in grads:
                @pl.loop(1, groups)
                def _(step):
                    other = lax.rem(column + step, groups)
                    along_copy(kind, other, other, block).wait_recv()

                total = grad[own_rows(2 * block + parity), own_cols(column)]
                for step in range(1, groups):
                    other = lax.rem(column + step, groups)
                    total = total + along[kind, other, own_rows(block), :].astype(jnp.float32)
                grad[own_rows(2 * block + parity), own_cols(column)] = total
                summed[kind, block] = total.astype(jnp.bfloat16)

        @pl.loop(1, half)
        def _(step):
            for kind in range(2):
                across_copy(kind, lax.rem(chip + step, half), chip).start()

    def finish_sums():
        @pl.loop(1, half)
        def _(step):
            other = lax.rem(chip + step, half)
            for kind in range(2):
                across_copy(kind, other, other).wait_recv()

        for kind, out, grad, blocks in ((0, out_r, grad_r, right_blocks), (1, out_l, grad_l, left_blocks)):
            side = width // blocks.shape[0]
            total = grad[own_rows(me), own_cols(column)]
            for step in range(1, half):
                total = total + across[kind, lax.rem(chip + step, half)].astype(jnp.float32)
            for right_of in range(cols // side):
                there = slice(right_of * side, (right_of + 1) * side)
                keep = blocks[me * rows // side, column * (cols // side) + right_of].astype(jnp.float32)
                out[:, there] = total[:, there] * keep / scales[kind]

    def wait_sums_sent():
        @pl.loop(0, half)
        def _(block):
            for kind, grad in grads:
                pair_copy(kind, grad, block).wait_send()

                @pl.loop(1, groups)
                def _(step):
                    along_copy(kind, lax.rem(column + step, groups), column, block).wait_send()

        @pl.loop(1, half)
        def _(step):
            for kind in range(2):
                across_copy(kind, lax.rem(chip + step, half), chip).wait_send()

    fetched = (
        pltpu.make_async_copy(right_in, right, load_sem.at[2]),
        pltpu.make_async_copy(left_in, left, load_sem.at[3]),
    )
    send_first()
    if parts > 1:
        load(1, 0, signal).start()
    for copy in fetched:
        copy.start()
    if parts > 1:
        send_in(1)
    if parts > 2:
        load(2, 0, signal).start()
    for copy in fetched:
        copy.wait()
    grad_r[...] = jnp.zeros_like(grad_r)
    grad_l[...] = jnp.zeros_like(grad_l)
    apply_mask(right_blocks, right)
    apply_mask(left_blocks, left)

    @pl.loop(0, parts)
    def _(part):
        wait_in(part)

        @pl.when(part + 2 < parts)
        def _():
            wait_in_sent(part)
            send_in(part + 2)

        @pl.when(part + 3 < parts)
        def _():
            load(part + 3, 0, signal).start()

        fetch(part)
        compute()

        @pl.when(part == last)
        def _():
            start_pairs()

        store(part)

        @pl.when(part < last)
        def _():
            send_out(part)

    send_last()
    send_along()
    for part in range(last):
        if part == last - 1:
            send_across()
        turn_out(part)
    if last == 0:
        send_across()
    finish_sums()
    turn_last()
    wait_sums_sent()

    @pl.loop(max(parts - 2, 0), parts)
    def _(part):
        wait_in_sent(part)

    wait_out_sent()


def hand_over(mixed, grad, right, left, out_m, out_g, out_r, out_l, sems):
    cuts = sems.shape[1]
    copies = []
    for kind, (source, target) in enumerate(((mixed, out_m), (grad, out_g), (right, out_r), (left, out_l))):
        step = source.shape[0] // cuts
        for cut in range(cuts):
            here = pl.ds(cut * step, step)
            copies.append(pltpu.make_async_copy(source.at[here], target.at[here], sems.at[kind, cut]))
    for copy in copies:
        copy.start()
    for copy in copies:
        copy.wait()


def shards_by_channel(signal, cotangent, right_factor, left_factor, right_blocks, left_blocks):
    rows_here, chans, width_two = signal.shape
    width_one = left_factor.shape[0]
    peers = lax.axis_size("seq")
    groups = lax.axis_size("ch")
    parts = chans // peers
    half = peers // 2
    cols = width_two // groups
    chunks = 4
    square = (width_one, width_two)
    scales = (math.sqrt(width_one * chans * groups), math.sqrt(width_two * chans * groups))
    hbm = pl.BlockSpec(memory_space=pl.ANY)
    vmem = pl.BlockSpec(memory_space=pltpu.VMEM)
    smem = pl.BlockSpec(memory_space=pltpu.SMEM)
    held = jax.ShapeDtypeStruct((parts, *square), jnp.bfloat16)
    landed = jax.ShapeDtypeStruct((chans, rows_here, width_two), jnp.bfloat16)
    results = ((signal.shape, jnp.bfloat16), (signal.shape, jnp.bfloat16))
    results = results + (((rows_here, cols), jnp.float32), ((rows_here, cols), jnp.float32))
    made = pl.pallas_call(
        functools.partial(mix_kernel, peers, groups, parts, chunks, scales),
        out_shape=tuple(pltpu.VMEM(*result) for result in results) + (held, held, landed, landed),
        in_specs=[smem, smem, hbm, hbm, hbm, hbm],
        out_specs=(vmem,) * 4 + (hbm,) * 4,
        scratch_shapes=[
            pltpu.VMEM(square, jnp.bfloat16),
            pltpu.VMEM(square, jnp.bfloat16),
            pltpu.VMEM(square, jnp.float32),
            pltpu.VMEM(square, jnp.float32),
            pltpu.VMEM(square, jnp.bfloat16),
            pltpu.VMEM(square, jnp.bfloat16),
            pltpu.VMEM(square, jnp.bfloat16),
            pltpu.VMEM(square, jnp.bfloat16),
            pltpu.VMEM(square, jnp.bfloat16),
            pltpu.VMEM((2, half, rows_here, width_two), jnp.float32),
            pltpu.VMEM((2, groups, half * rows_here, cols), jnp.bfloat16),
            pltpu.VMEM((2, half, rows_here, cols), jnp.bfloat16),
            pltpu.VMEM((2, half, rows_here, cols), jnp.bfloat16),
            pltpu.VMEM((rows_here, peers, width_two), jnp.bfloat16),
            pltpu.VMEM((peers, rows_here, width_two), jnp.bfloat16),
            pltpu.VMEM((2, 2, peers, rows_here, width_two), jnp.bfloat16),
            pltpu.SemaphoreType.DMA((4, parts, peers)),
            pltpu.SemaphoreType.DMA((4, parts, peers)),
            pltpu.SemaphoreType.DMA((2, parts)),
            pltpu.SemaphoreType.DMA((4,)),
            pltpu.SemaphoreType.DMA((2, chunks, peers)),
            pltpu.SemaphoreType.DMA((2, chunks, peers)),
            pltpu.SemaphoreType.DMA((2, 2, half)),
            pltpu.SemaphoreType.DMA((2, 2, groups, half)),
            pltpu.SemaphoreType.DMA((2, 2, half)),
            pltpu.SemaphoreType.DMA((4,)),
        ],
        compiler_params=pltpu.CompilerParams(
            collective_id=0, has_side_effects=True, vmem_limit_bytes=47 * 2**20
        ),
    )(right_blocks, left_blocks, signal, cotangent, right_factor, left_factor)
    made = [pltpu.with_memory_space_constraint(array, pltpu.VMEM) for array in made[:4]]
    return pl.pallas_call(
        hand_over,
        out_shape=tuple(jax.ShapeDtypeStruct(*result) for result in results),
        in_specs=[vmem] * 4,
        out_specs=(hbm,) * 4,
        scratch_shapes=[pltpu.SemaphoreType.DMA((4, 8))],
        compiler_params=pltpu.CompilerParams(vmem_limit_bytes=8 * 2**20),
    )(*made)


def shards(signal, *others):
    rows_here, chans, width_two = signal.shape
    peers = lax.axis_size("seq")
    width_one = others[1].shape[0]
    sides = (width_two // others[3].shape[0], width_one // others[4].shape[0])
    fits = chans % peers == 0 and rows_here % 16 == 0 and peers % 2 == 0
    fits = fits and sides == (128, 128) and rows_here == 128
    fits = fits and width_two // lax.axis_size("ch") % 128 == 0
    if fits and width_one == 1024 and width_two == 1024 and chans // peers <= 4:
        return shards_by_channel(signal, *others)
    return shards_by_column(signal, *others)


def solution(mesh):
    return jax.shard_map(
        shards,
        mesh=mesh,
        in_specs=(P("seq", "ch", None), P("seq", "ch", None), P(), P(), P(), P()),
        out_specs=(P("seq", "ch", None), P("seq", "ch", None), P("seq", "ch"), P("seq", "ch")),
        check_vma=False,
    )
```

```python
import functools
import math

import jax
import jax.numpy as jnp
from jax import lax
from jax.experimental import pallas as pl
from jax.experimental.pallas import tpu as pltpu
from jax.sharding import PartitionSpec as P


def expand(blocks, width):
    tile = width // blocks.shape[0]
    return jnp.repeat(jnp.repeat(blocks, tile, axis=0), tile, axis=1)


def to_columns(rows, peers):
    rows_here, chans, width_two = rows.shape
    piece = width_two // peers
    arranged = rows.reshape(rows_here, chans, peers, piece).transpose(0, 2, 1, 3)
    return arranged.reshape(rows_here, peers, chans * piece)


def to_rows(received, chans):
    rows_here, peers, wide = received.shape
    piece = wide // chans
    arranged = received.reshape(rows_here, peers, chans, piece).transpose(0, 2, 1, 3)
    return arranged.reshape(rows_here, chans, peers * piece)


def shards_by_column(signal, cotangent, right_factor, left_factor, right_blocks, left_blocks):
    rows_here, chans, width_two = signal.shape
    width_one = left_factor.shape[0]
    peers = lax.axis_size("seq")
    right_mask = expand(right_blocks, width_two).astype(jnp.bfloat16)
    left_mask = expand(left_blocks, width_one).astype(jnp.bfloat16)
    right_eff = right_factor * right_mask
    left_eff = left_factor * left_mask
    flat_signal = signal.reshape(rows_here * chans, width_two)
    first_rows = jnp.dot(flat_signal, right_eff.T, preferred_element_type=jnp.float32)
    first_rows = to_columns(
        first_rows.astype(jnp.bfloat16).reshape(rows_here, chans, width_two), peers
    )
    sig_f = signal.astype(jnp.float32)
    gate = jax.nn.sigmoid(sig_f)
    swish = sig_f * gate
    cot_f = cotangent.astype(jnp.float32)
    grad_rows = to_columns((cot_f * swish).astype(jnp.bfloat16), peers)
    z_cols = lax.all_to_all(first_rows, "seq", split_axis=1, concat_axis=0, tiled=True)
    flat_cols = z_cols.reshape(width_one, z_cols.shape[2])
    result = jnp.dot(left_eff, flat_cols, preferred_element_type=jnp.float32)
    y_cols = result.astype(jnp.bfloat16).reshape(width_one, 1, z_cols.shape[2])
    y_back = lax.all_to_all(y_cols, "seq", split_axis=0, concat_axis=1, tiled=True)
    dy_cols = lax.all_to_all(grad_rows, "seq", split_axis=1, concat_axis=0, tiled=True)
    flat_cols = dy_cols.reshape(width_one, dy_cols.shape[2])
    result = lax.dot_general(
        left_eff, flat_cols, (((0,), (0,)), ((), ())), preferred_element_type=jnp.float32
    )
    dz_cols = result.astype(jnp.bfloat16).reshape(width_one, 1, dy_cols.shape[2])
    dz_back = lax.all_to_all(dz_cols, "seq", split_axis=0, concat_axis=1, tiled=True)
    y_rows = to_rows(y_back, chans)
    dz_rows = to_rows(dz_back, chans)
    y_f = y_rows.astype(jnp.float32)
    mixed = (sig_f + y_f * swish).astype(jnp.bfloat16)
    dz_flat = dz_rows.reshape(rows_here * chans, width_two)
    back = jnp.dot(dz_flat, right_eff, preferred_element_type=jnp.float32).reshape(
        rows_here, chans, width_two
    )
    dswish = gate * (1.0 + sig_f * (1.0 - gate))
    grad_signal = (cot_f * (1.0 + y_f * dswish) + back).astype(jnp.bfloat16)
    wide = z_cols.shape[2]
    z_flat = z_cols.reshape(width_one, wide)
    dy_flat = dy_cols.reshape(width_one, wide)
    left_term = lax.dot_general(
        dy_flat, z_flat, (((1,), (1,)), ((), ())), preferred_element_type=jnp.float32
    )
    right_term = lax.dot_general(
        dz_flat, flat_signal, (((0,), (0,)), ((), ())), preferred_element_type=jnp.float32
    )
    total_chans = chans * lax.axis_size("ch")
    right_term = right_term * right_mask.astype(jnp.float32) / math.sqrt(width_one * total_chans)
    left_term = left_term * left_mask.astype(jnp.float32) / math.sqrt(width_two * total_chans)
    partial_value = (
        lax.psum_scatter(right_term, "seq", scatter_dimension=0, tiled=True),
        lax.psum_scatter(left_term, "seq", scatter_dimension=0, tiled=True),
    )
    grad_right, grad_left = (
        lax.psum_scatter(partial_value[0], "ch", scatter_dimension=1, tiled=True),
        lax.psum_scatter(partial_value[1], "ch", scatter_dimension=1, tiled=True),
    )
    return (mixed, grad_signal, grad_right, grad_left)


def mix_kernel(
    peers, groups, parts, chunks, scales, right_blocks, left_blocks, signal, cotangent, right_in, left_in,
    out_m, out_g, out_r, out_l, xh, ch, mt, gt,
    right, left, grad_r, grad_l, xbuf, cbuf, zbuf, dybuf, dzbuf, pairs, along, summed, across, slab, facing, turned,
    send_sem, recv_sem, own_in_sem, stage_sem, last_send, last_recv, pair_sems, along_sems, across_sems, load_sem, first_sem,
    free_sem,
):
    me = lax.axis_index("seq")
    column = lax.axis_index("ch")
    rows = signal.shape[0]
    width = signal.shape[2]
    order = left.shape[0]
    tile = 256
    piece = rows // chunks
    last = parts - 1
    others = peers - 1
    spare = parts % 2

    def own_rows(who):
        return pl.ds(pl.multiple_of(who * rows, rows), rows)

    def some_rows(who, chunk):
        return pl.ds(pl.multiple_of(who * rows + chunk * piece, piece), piece)

    def remote(source, target, going, coming, who):
        return pltpu.make_async_remote_copy(
            src_ref=source,
            dst_ref=target,
            send_sem=going,
            recv_sem=coming,
            device_id=(who, column),
            device_id_type=pl.DeviceIdType.MESH,
        )

    def take_all(ref, sem):
        pltpu.make_async_copy(ref, ref, sem).wait()

    def each_peer(action):
        @pl.loop(1, peers)
        def _(step):
            action(lax.rem(me + step, peers))

    barrier = pltpu.get_barrier_semaphore()

    def load(part, kind, source):
        there = pl.ds(pl.multiple_of(part * peers, peers), peers)
        return pltpu.make_async_copy(source.at[:, there, :], slab, load_sem.at[kind])

    def first_load(chunk):
        here = pl.ds(chunk * piece, piece)
        return pltpu.make_async_copy(signal.at[here, pl.ds(0, peers), :], slab.at[here], first_sem.at[chunk])

    for chunk in range(chunks):
        first_load(chunk).start()

    def greet(who):
        pl.semaphore_signal(
            barrier, inc=1, device_id=(who, column), device_id_type=pl.DeviceIdType.MESH
        )

    each_peer(greet)

    @pl.loop(1, groups)
    def _(step):
        pl.semaphore_signal(
            barrier,
            inc=1,
            device_id=(me, lax.rem(column + step, groups)),
            device_id_type=pl.DeviceIdType.MESH,
        )

    inputs = ((0, signal, xh), (1, cotangent, ch))
    outputs = ((2, mt, xh, xbuf, out_m), (3, gt, ch, cbuf, out_g))

    def turn(part, kind, chunk, count):
        @pl.loop(chunk * (piece // 16), (chunk + count) * (piece // 16))
        def _(step):
            here = pl.ds(pl.multiple_of(step * 16, 16), 16)
            turned[lax.rem(part, 2), kind, :, here, :] = jnp.swapaxes(slab[here], 0, 1)

    def in_copy(kind, part, held, who, at_rows, there):
        return remote(
            turned.at[lax.rem(part, 2), kind, who, at_rows],
            held.at[part, there],
            send_sem.at[kind, part],
            recv_sem.at[kind, part],
            who,
        )

    def whole_in_copy(kind, part, held, who):
        return in_copy(kind, part, held, who, pl.ds(0, rows), own_rows(me))

    def own_copy(kind, part, held):
        return pltpu.make_async_copy(
            turned.at[lax.rem(part, 2), kind, me], held.at[part, own_rows(me)], own_in_sem.at[kind, part]
        )

    def send_in(part):
        for kind, source, held in inputs:
            load(part, kind, source).wait()
            turn(part, kind, 0, chunks)
            if kind == 0:
                load(part, 1, cotangent).start()
            each_peer(lambda who: whole_in_copy(kind, part, held, who).start())
            own_copy(kind, part, held).start()

    def send_first():
        for kind, source, held in inputs:
            if kind == 1:
                load(0, kind, source).wait()
            for chunk in range(chunks):
                if kind == 0:
                    first_load(chunk).wait()
                turn(0, kind, chunk, 1)
                if kind == 0 and chunk == 0:
                    pl.semaphore_wait(barrier, peers - 1 + groups - 1)
                each_peer(
                    lambda who: in_copy(
                        kind, 0, held, who, pl.ds(chunk * piece, piece), some_rows(me, chunk)
                    ).start()
                )
            if kind == 0:
                load(0, 1, cotangent).start()
            own_copy(kind, 0, held).start()

    def wait_in(part):
        for kind, source, held in inputs:
            take_all(held.at[part, pl.ds(0, others * rows)], recv_sem.at[kind, part])
            own_copy(kind, part, held).wait()

    def wait_in_sent(part):
        for kind, source, held in inputs:
            take_all(turned.at[lax.rem(part, 2), kind, pl.ds(0, others)], send_sem.at[kind, part])

    def fetch(part):
        copies = [
            pltpu.make_async_copy(held.at[part], buf, stage_sem.at[kind - 2])
            for kind, landed, held, buf, out in outputs
        ]
        for copy in copies:
            copy.start()
        for copy in copies:
            copy.wait()

    def store(part):
        copies = []
        for kind, landed, held, buf, out in outputs:
            copies.append(pltpu.make_async_copy(buf, held.at[part], stage_sem.at[kind - 2]))
            copies.append(
                pltpu.make_async_copy(buf.at[own_rows(me)], landed.at[part * peers + me], stage_sem.at[kind])
            )
        for copy in copies:
            copy.start()
        for copy in copies:
            copy.wait()

    def send_out(part):
        def one(who):
            for kind, landed, held, buf, out in outputs:
                remote(
                    held.at[part, own_rows(who)], landed.at[part * peers + me],
                    send_sem.at[kind, part], recv_sem.at[kind, part], who,
                ).start()

        each_peer(one)

    def send_last():
        for chunk in range(chunks):
            for kind, landed, held, buf, out in outputs:
                each_peer(
                    lambda who: remote(
                        held.at[last, some_rows(who, chunk)],
                        turned.at[spare, kind - 2, me, pl.ds(chunk * piece, piece)],
                        last_send.at[kind - 2], last_recv.at[kind - 2, chunk], who,
                    ).start()
                )

    def turn_out(part):
        for kind, landed, held, buf, out in outputs:
            take_all(landed.at[pl.ds(part * peers, others)], recv_sem.at[kind, part])
            copy = pltpu.make_async_copy(landed.at[pl.ds(part * peers, peers)], facing, stage_sem.at[0])
            copy.start()
            copy.wait()

            @pl.loop(0, rows // 16)
            def _(step):
                here = pl.ds(pl.multiple_of(step * 16, 16), 16)
                out[here, part * peers:(part + 1) * peers, :] = jnp.swapaxes(facing[:, here, :], 0, 1)

    def keep_own():
        for kind, landed, held, buf, out in outputs:
            turned[spare, kind - 2, me] = buf[own_rows(me), :]

    def turn_last():
        for chunk in range(chunks):
            for kind, landed, held, buf, out in outputs:
                take_all(
                    turned.at[spare, kind - 2, pl.ds(0, others), pl.ds(chunk * piece, piece)],
                    last_recv.at[kind - 2, chunk],
                )

                @pl.loop(chunk * (piece // 16), (chunk + 1) * (piece // 16))
                def _(step):
                    here = pl.ds(pl.multiple_of(step * 16, 16), 16)
                    out[here, last * peers:parts * peers, :] = jnp.swapaxes(
                        turned[spare, kind - 2, :, here, :], 0, 1
                    )

    def wait_out_sent(part):
        for kind, landed, held, buf, out in outputs:
            take_all(held.at[part, pl.ds(0, others * rows)], send_sem.at[kind, part])

    def wait_last_sent():
        for kind, landed, held, buf, out in outputs:
            take_all(held.at[last, pl.ds(0, others * rows)], last_send.at[kind - 2])

    def at(step):
        return pl.ds(pl.multiple_of(step * tile, tile), tile)

    def dot(a, b, dims):
        return lax.dot_general(a, b, (dims, ((), ())), preferred_element_type=jnp.float32)

    def compute():
        @pl.loop(0, order // tile)
        def _(step):
            x = xbuf[at(step), :]
            zbuf[at(step), :] = dot(x, right[...], ((1,), (1,))).astype(jnp.bfloat16)
            sig = x.astype(jnp.float32)
            swish = sig * jax.nn.sigmoid(sig)
            cot = cbuf[at(step), :].astype(jnp.float32)
            dybuf[at(step), :] = (cot * swish).astype(jnp.bfloat16)

        @pl.loop(0, order // tile)
        def _(step):
            dzbuf[at(step), :] = dot(left[:, at(step)], dybuf[...], ((0,), (0,))).astype(jnp.bfloat16)
            grad_l[at(step), :] += dot(dybuf[at(step), :], zbuf[...], ((1,), (1,)))

        @pl.loop(0, width // tile)
        def _(step):
            grad_r[at(step), :] += dot(dzbuf[:, at(step)], xbuf[...], ((0,), (0,)))

        @pl.loop(0, order // tile)
        def _(step):
            y = dot(left[at(step), :], zbuf[...], ((1,), (0,))).astype(jnp.bfloat16).astype(jnp.float32)
            back = dot(dzbuf[at(step), :], right[...], ((1,), (0,)))
            sig = xbuf[at(step), :].astype(jnp.float32)
            cot = cbuf[at(step), :].astype(jnp.float32)
            gate = jax.nn.sigmoid(sig)
            xbuf[at(step), :] = (sig + y * (sig * gate)).astype(jnp.bfloat16)
            dswish = gate * (1.0 + sig * (1.0 - gate))
            cbuf[at(step), :] = (cot * (1.0 + y * dswish) + back).astype(jnp.bfloat16)

    def apply_mask(blocks, target):
        side = target.shape[0] // blocks.shape[0]

        @pl.loop(0, blocks.shape[0])
        def _(down):
            here = pl.ds(pl.multiple_of(down * side, side), side)
            for right_of in range(blocks.shape[1]):
                there = slice(right_of * side, (right_of + 1) * side)
                keep = blocks[down, right_of].astype(jnp.float32)
                target[here, there] = (target[here, there].astype(jnp.float32) * keep).astype(jnp.bfloat16)

    half = peers // 2
    parity = lax.rem(me, 2)
    chip = me // 2
    sibling = me + 1 - 2 * parity
    cols = width // groups
    grads = ((0, grad_r), (1, grad_l))

    def pair_copy(kind, grad, block):
        return remote(
            grad.at[own_rows(2 * block + 1 - parity)], pairs.at[kind, block],
            pair_sems.at[0, kind, block], pair_sems.at[1, kind, block], sibling,
        )

    def own_cols(line):
        return pl.ds(pl.multiple_of(line * cols, cols), cols)

    def along_copy(kind, other, slot, block):
        return pltpu.make_async_remote_copy(
            src_ref=zbuf.at[own_rows(kind * half + block), own_cols(other)],
            dst_ref=along.at[kind, slot, own_rows(block)],
            send_sem=along_sems.at[0, kind, other, block],
            recv_sem=along_sems.at[1, kind, slot, block],
            device_id=(me, other),
            device_id_type=pl.DeviceIdType.MESH,
        )

    def across_copy(kind, other, slot):
        return remote(
            summed.at[kind, other], across.at[kind, slot],
            across_sems.at[0, kind, other], across_sems.at[1, kind, slot], 2 * other + parity,
        )

    def start_pairs():
        @pl.loop(0, half)
        def _(block):
            for kind, grad in grads:
                pair_copy(kind, grad, block).start()

    def send_along():
        @pl.loop(0, half)
        def _(block):
            for kind, grad in grads:
                pair_copy(kind, grad, block).wait_recv()
                total = grad[own_rows(2 * block + parity), :] + pairs[kind, block]
                grad[own_rows(2 * block + parity), :] = total
                zbuf[own_rows(kind * half + block), :] = total.astype(jnp.bfloat16)

                @pl.loop(1, groups)
                def _(step):
                    along_copy(kind, lax.rem(column + step, groups), column, block).start()

    def send_across():
        @pl.loop(0, half)
        def _(block):
            for kind, grad in grads:
                @pl.loop(1, groups)
                def _(step):
                    other = lax.rem(column + step, groups)
                    along_copy(kind, other, other, block).wait_recv()

                total = grad[own_rows(2 * block + parity), own_cols(column)]
                for step in range(1, groups):
                    other = lax.rem(column + step, groups)
                    total = total + along[kind, other, own_rows(block), :].astype(jnp.float32)
                grad[own_rows(2 * block + parity), own_cols(column)] = total
                summed[kind, block] = total.astype(jnp.bfloat16)

        @pl.loop(1, half)
        def _(step):
            for kind in range(2):
                across_copy(kind, lax.rem(chip + step, half), chip).start()

    def finish_sums():
        @pl.loop(1, half)
        def _(step):
            other = lax.rem(chip + step, half)
            for kind in range(2):
                across_copy(kind, other, other).wait_recv()

        for kind, out, grad, blocks in ((0, out_r, grad_r, right_blocks), (1, out_l, grad_l, left_blocks)):
            side = width // blocks.shape[0]
            total = grad[own_rows(me), own_cols(column)]
            for step in range(1, half):
                total = total + across[kind, lax.rem(chip + step, half)].astype(jnp.float32)
            for right_of in range(cols // side):
                there = slice(right_of * side, (right_of + 1) * side)
                keep = blocks[me * rows // side, column * (cols // side) + right_of].astype(jnp.float32)
                out[:, there] = total[:, there] * keep / scales[kind]

    def wait_sums_sent():
        @pl.loop(0, half)
        def _(block):
            for kind, grad in grads:
                pair_copy(kind, grad, block).wait_send()

                @pl.loop(1, groups)
                def _(step):
                    along_copy(kind, lax.rem(column + step, groups), column, block).wait_send()

    def wait_across_sent():
        @pl.loop(1, half)
        def _(step):
            for kind in range(2):
                across_copy(kind, lax.rem(chip + step, half), chip).wait_send()

    def tell_free():
        def one(who):
            pl.semaphore_signal(
                free_sem, inc=1, device_id=(who, column), device_id_type=pl.DeviceIdType.MESH
            )

        each_peer(one)

    fetched = (
        pltpu.make_async_copy(right_in, right, load_sem.at[2]),
        pltpu.make_async_copy(left_in, left, load_sem.at[3]),
    )
    send_first()
    if parts > 1:
        load(1, 0, signal).start()
    for copy in fetched:
        copy.start()
    if parts > 1:
        send_in(1)
    if parts > 2:
        load(2, 0, signal).start()
    for copy in fetched:
        copy.wait()
    grad_r[...] = jnp.zeros_like(grad_r)
    grad_l[...] = jnp.zeros_like(grad_l)
    apply_mask(right_blocks, right)
    apply_mask(left_blocks, left)

    @pl.loop(0, parts)
    def _(part):
        wait_in(part)

        @pl.when(part + 2 < parts)
        def _():
            wait_in_sent(part)
            send_in(part + 2)

        @pl.when(part + 3 < parts)
        def _():
            load(part + 3, 0, signal).start()

        @pl.when(part == last)
        def _():
            if parts > 1:
                wait_in_sent(last - 1)
            tell_free()

        fetch(part)
        compute()

        @pl.when(part == last)
        def _():
            start_pairs()

        store(part)

        @pl.when(part < last)
        def _():
            send_out(part)

    pl.semaphore_wait(free_sem, others)
    send_last()
    keep_own()
    send_along()
    if last > 0:
        turn_out(0)
    send_across()
    for part in range(1, last):
        turn_out(part)
    wait_in_sent(last)
    for part in range(last):
        wait_out_sent(part)
    wait_sums_sent()
    turn_last()
    finish_sums()
    wait_across_sent()
    wait_last_sent()


def hand_over(mixed, grad, right, left, out_m, out_g, out_r, out_l, sems):
    cuts = sems.shape[1]
    copies = []
    for kind, (source, target) in enumerate(((mixed, out_m), (grad, out_g), (right, out_r), (left, out_l))):
        step = source.shape[0] // cuts
        for cut in range(cuts):
            here = pl.ds(cut * step, step)
            copies.append(pltpu.make_async_copy(source.at[here], target.at[here], sems.at[kind, cut]))
    for copy in copies:
        copy.start()
    for copy in copies:
        copy.wait()


def shards_by_channel(signal, cotangent, right_factor, left_factor, right_blocks, left_blocks):
    rows_here, chans, width_two = signal.shape
    width_one = left_factor.shape[0]
    peers = lax.axis_size("seq")
    groups = lax.axis_size("ch")
    parts = chans // peers
    half = peers // 2
    cols = width_two // groups
    chunks = 4
    square = (width_one, width_two)
    scales = (math.sqrt(width_one * chans * groups), math.sqrt(width_two * chans * groups))
    hbm = pl.BlockSpec(memory_space=pl.ANY)
    vmem = pl.BlockSpec(memory_space=pltpu.VMEM)
    smem = pl.BlockSpec(memory_space=pltpu.SMEM)
    held = jax.ShapeDtypeStruct((parts, *square), jnp.bfloat16)
    landed = jax.ShapeDtypeStruct((chans, rows_here, width_two), jnp.bfloat16)
    results = ((signal.shape, jnp.bfloat16), (signal.shape, jnp.bfloat16))
    results = results + (((rows_here, cols), jnp.float32), ((rows_here, cols), jnp.float32))
    made = pl.pallas_call(
        functools.partial(mix_kernel, peers, groups, parts, chunks, scales),
        out_shape=tuple(pltpu.VMEM(*result) for result in results) + (held, held, landed, landed),
        in_specs=[smem, smem, hbm, hbm, hbm, hbm],
        out_specs=(vmem,) * 4 + (hbm,) * 4,
        scratch_shapes=[
            pltpu.VMEM(square, jnp.bfloat16),
            pltpu.VMEM(square, jnp.bfloat16),
            pltpu.VMEM(square, jnp.float32),
            pltpu.VMEM(square, jnp.float32),
            pltpu.VMEM(square, jnp.bfloat16),
            pltpu.VMEM(square, jnp.bfloat16),
            pltpu.VMEM(square, jnp.bfloat16),
            pltpu.VMEM(square, jnp.bfloat16),
            pltpu.VMEM(square, jnp.bfloat16),
            pltpu.VMEM((2, half, rows_here, width_two), jnp.float32),
            pltpu.VMEM((2, groups, half * rows_here, cols), jnp.bfloat16),
            pltpu.VMEM((2, half, rows_here, cols), jnp.bfloat16),
            pltpu.VMEM((2, half, rows_here, cols), jnp.bfloat16),
            pltpu.VMEM((rows_here, peers, width_two), jnp.bfloat16),
            pltpu.VMEM((peers, rows_here, width_two), jnp.bfloat16),
            pltpu.VMEM((2, 2, peers, rows_here, width_two), jnp.bfloat16),
            pltpu.SemaphoreType.DMA((4, parts)),
            pltpu.SemaphoreType.DMA((4, parts)),
            pltpu.SemaphoreType.DMA((2, parts)),
            pltpu.SemaphoreType.DMA((4,)),
            pltpu.SemaphoreType.DMA((2,)),
            pltpu.SemaphoreType.DMA((2, chunks)),
            pltpu.SemaphoreType.DMA((2, 2, half)),
            pltpu.SemaphoreType.DMA((2, 2, groups, half)),
            pltpu.SemaphoreType.DMA((2, 2, half)),
            pltpu.SemaphoreType.DMA((4,)),
            pltpu.SemaphoreType.DMA((chunks,)),
            pltpu.SemaphoreType.REGULAR,
        ],
        compiler_params=pltpu.CompilerParams(
            collective_id=0, has_side_effects=True, vmem_limit_bytes=47 * 2**20
        ),
    )(right_blocks, left_blocks, signal, cotangent, right_factor, left_factor)
    made = [pltpu.with_memory_space_constraint(array, pltpu.VMEM) for array in made[:4]]
    return pl.pallas_call(
        hand_over,
        out_shape=tuple(jax.ShapeDtypeStruct(*result) for result in results),
        in_specs=[vmem] * 4,
        out_specs=(hbm,) * 4,
        scratch_shapes=[pltpu.SemaphoreType.DMA((4, 8))],
        compiler_params=pltpu.CompilerParams(vmem_limit_bytes=8 * 2**20),
    )(*made)


def shards(signal, *others):
    rows_here, chans, width_two = signal.shape
    peers = lax.axis_size("seq")
    width_one = others[1].shape[0]
    sides = (width_two // others[3].shape[0], width_one // others[4].shape[0])
    fits = chans % peers == 0 and rows_here % 16 == 0 and peers % 2 == 0
    fits = fits and sides == (128, 128) and rows_here == 128
    fits = fits and width_two // lax.axis_size("ch") % 128 == 0
    if fits and width_one == 1024 and width_two == 1024 and chans // peers <= 4:
        return shards_by_channel(signal, *others)
    return shards_by_column(signal, *others)


def solution(mesh):
    return jax.shard_map(
        shards,
        mesh=mesh,
        in_specs=(P("seq", "ch", None), P("seq", "ch", None), P(), P(), P(), P()),
        out_specs=(P("seq", "ch", None), P("seq", "ch", None), P("seq", "ch"), P("seq", "ch")),
        check_vma=False,
    )
```

```python
import functools
import math

import jax
import jax.numpy as jnp
from jax import lax
from jax.experimental import pallas as pl
from jax.experimental.pallas import tpu as pltpu
from jax.sharding import PartitionSpec as P


def expand(blocks, width):
    tile = width // blocks.shape[0]
    return jnp.repeat(jnp.repeat(blocks, tile, axis=0), tile, axis=1)


def to_columns(rows, peers):
    rows_here, chans, width_two = rows.shape
    piece = width_two // peers
    arranged = rows.reshape(rows_here, chans, peers, piece).transpose(0, 2, 1, 3)
    return arranged.reshape(rows_here, peers, chans * piece)


def to_rows(received, chans):
    rows_here, peers, wide = received.shape
    piece = wide // chans
    arranged = received.reshape(rows_here, peers, chans, piece).transpose(0, 2, 1, 3)
    return arranged.reshape(rows_here, chans, peers * piece)


def shards_by_column(signal, cotangent, right_factor, left_factor, right_blocks, left_blocks):
    rows_here, chans, width_two = signal.shape
    width_one = left_factor.shape[0]
    peers = lax.axis_size("seq")
    right_mask = expand(right_blocks, width_two).astype(jnp.bfloat16)
    left_mask = expand(left_blocks, width_one).astype(jnp.bfloat16)
    right_eff = right_factor * right_mask
    left_eff = left_factor * left_mask
    flat_signal = signal.reshape(rows_here * chans, width_two)
    first_rows = jnp.dot(flat_signal, right_eff.T, preferred_element_type=jnp.float32)
    first_rows = to_columns(
        first_rows.astype(jnp.bfloat16).reshape(rows_here, chans, width_two), peers
    )
    sig_f = signal.astype(jnp.float32)
    gate = jax.nn.sigmoid(sig_f)
    swish = sig_f * gate
    cot_f = cotangent.astype(jnp.float32)
    grad_rows = to_columns((cot_f * swish).astype(jnp.bfloat16), peers)
    z_cols = lax.all_to_all(first_rows, "seq", split_axis=1, concat_axis=0, tiled=True)
    flat_cols = z_cols.reshape(width_one, z_cols.shape[2])
    result = jnp.dot(left_eff, flat_cols, preferred_element_type=jnp.float32)
    y_cols = result.astype(jnp.bfloat16).reshape(width_one, 1, z_cols.shape[2])
    y_back = lax.all_to_all(y_cols, "seq", split_axis=0, concat_axis=1, tiled=True)
    dy_cols = lax.all_to_all(grad_rows, "seq", split_axis=1, concat_axis=0, tiled=True)
    flat_cols = dy_cols.reshape(width_one, dy_cols.shape[2])
    result = lax.dot_general(
        left_eff, flat_cols, (((0,), (0,)), ((), ())), preferred_element_type=jnp.float32
    )
    dz_cols = result.astype(jnp.bfloat16).reshape(width_one, 1, dy_cols.shape[2])
    dz_back = lax.all_to_all(dz_cols, "seq", split_axis=0, concat_axis=1, tiled=True)
    y_rows = to_rows(y_back, chans)
    dz_rows = to_rows(dz_back, chans)
    y_f = y_rows.astype(jnp.float32)
    mixed = (sig_f + y_f * swish).astype(jnp.bfloat16)
    dz_flat = dz_rows.reshape(rows_here * chans, width_two)
    back = jnp.dot(dz_flat, right_eff, preferred_element_type=jnp.float32).reshape(
        rows_here, chans, width_two
    )
    dswish = gate * (1.0 + sig_f * (1.0 - gate))
    grad_signal = (cot_f * (1.0 + y_f * dswish) + back).astype(jnp.bfloat16)
    wide = z_cols.shape[2]
    z_flat = z_cols.reshape(width_one, wide)
    dy_flat = dy_cols.reshape(width_one, wide)
    left_term = lax.dot_general(
        dy_flat, z_flat, (((1,), (1,)), ((), ())), preferred_element_type=jnp.float32
    )
    right_term = lax.dot_general(
        dz_flat, flat_signal, (((0,), (0,)), ((), ())), preferred_element_type=jnp.float32
    )
    total_chans = chans * lax.axis_size("ch")
    right_term = right_term * right_mask.astype(jnp.float32) / math.sqrt(width_one * total_chans)
    left_term = left_term * left_mask.astype(jnp.float32) / math.sqrt(width_two * total_chans)
    partial_value = (
        lax.psum_scatter(right_term, "seq", scatter_dimension=0, tiled=True),
        lax.psum_scatter(left_term, "seq", scatter_dimension=0, tiled=True),
    )
    grad_right, grad_left = (
        lax.psum_scatter(partial_value[0], "ch", scatter_dimension=1, tiled=True),
        lax.psum_scatter(partial_value[1], "ch", scatter_dimension=1, tiled=True),
    )
    return (mixed, grad_signal, grad_right, grad_left)


def mix_kernel(peers, groups, parts, chunks, scales, *refs):
    right_blocks, left_blocks, signal, cotangent, right_in, left_in, *refs = refs
    out_m, out_g, xh, ch, mt, gt, kept, *refs = refs
    away, refs = refs[:peers // 2 - 1], refs[peers // 2 - 1:]
    right, left, grad_r, grad_l, xbuf, cbuf, zbuf, dybuf, dzbuf, *refs = refs
    pairs, along, summed, own_sum, slab, facing, turned, *refs = refs
    in_send, in_recv, own_in_sem, out_send, out_recv, last_recv, stage_sem, *refs = refs
    pair_sems, along_sems, sum_sem, load_sem, first_sem, free_sem = refs
    me = lax.axis_index("seq")
    column = lax.axis_index("ch")
    rows = signal.shape[0]
    width = signal.shape[2]
    order = left.shape[0]
    tile = 256
    piece = rows // chunks
    last = parts - 1
    others = peers - 1
    spare = parts % 2

    def own_rows(who):
        return pl.ds(pl.multiple_of(who * rows, rows), rows)

    def some_rows(who, chunk):
        return pl.ds(pl.multiple_of(who * rows + chunk * piece, piece), piece)

    def remote(source, target, going, coming, who):
        return pltpu.make_async_remote_copy(
            src_ref=source,
            dst_ref=target,
            send_sem=going,
            recv_sem=coming,
            device_id=(who, column),
            device_id_type=pl.DeviceIdType.MESH,
        )

    def take_all(ref, sem):
        pltpu.make_async_copy(ref, ref, sem).wait()

    def each_peer(action):
        @pl.loop(1, peers)
        def _(step):
            action(lax.rem(me + step, peers))

    barrier = pltpu.get_barrier_semaphore()

    def load(part, kind, source):
        there = pl.ds(pl.multiple_of(part * peers, peers), peers)
        return pltpu.make_async_copy(source.at[:, there, :], slab, load_sem.at[kind])

    def first_load(chunk):
        here = pl.ds(chunk * piece, piece)
        return pltpu.make_async_copy(signal.at[here, pl.ds(0, peers), :], slab.at[here], first_sem.at[chunk])

    for chunk in range(chunks):
        first_load(chunk).start()

    def greet(who):
        pl.semaphore_signal(
            barrier, inc=1, device_id=(who, column), device_id_type=pl.DeviceIdType.MESH
        )

    @pl.loop(1, groups)
    def _(step):
        pl.semaphore_signal(
            barrier,
            inc=1,
            device_id=(me, lax.rem(column + step, groups)),
            device_id_type=pl.DeviceIdType.MESH,
        )

    each_peer(greet)

    inputs = ((0, signal, xh), (1, cotangent, ch))
    outputs = ((2, mt, xh, xbuf, out_m), (3, gt, ch, cbuf, out_g))

    def turn(part, kind, chunk, count):
        @pl.loop(chunk * (piece // 16), (chunk + count) * (piece // 16))
        def _(step):
            here = pl.ds(pl.multiple_of(step * 16, 16), 16)
            turned[lax.rem(part, 2), kind, :, here, :] = jnp.swapaxes(slab[here], 0, 1)

    def in_copy(kind, part, held, who, at_rows, there):
        return remote(
            turned.at[lax.rem(part, 2), kind, who, at_rows],
            held.at[part, there],
            in_send.at[kind, lax.rem(part, 2)],
            in_recv.at[kind, part],
            who,
        )

    def whole_in_copy(kind, part, held, who):
        return in_copy(kind, part, held, who, pl.ds(0, rows), own_rows(me))

    def own_copy(kind, part, held):
        return pltpu.make_async_copy(
            turned.at[lax.rem(part, 2), kind, me], held.at[part, own_rows(me)], own_in_sem.at[kind, lax.rem(part, 2)]
        )

    def send_in(part):
        for kind, source, held in inputs:
            load(part, kind, source).wait()
            turn(part, kind, 0, chunks)
            if kind == 0:
                load(part, 1, cotangent).start()
            each_peer(lambda who: whole_in_copy(kind, part, held, who).start())
            own_copy(kind, part, held).start()

    def send_first():
        for kind, source, held in inputs:
            if kind == 1:
                load(0, kind, source).wait()
            for chunk in range(chunks):
                if kind == 0:
                    first_load(chunk).wait()
                turn(0, kind, chunk, 1)
                if kind == 0 and chunk == 0:
                    pl.semaphore_wait(barrier, peers - 1 + groups - 1)
                each_peer(
                    lambda who: in_copy(
                        kind, 0, held, who, pl.ds(chunk * piece, piece), some_rows(me, chunk)
                    ).start()
                )
            if kind == 0:
                load(0, 1, cotangent).start()
            own_copy(kind, 0, held).start()

    def wait_in(part):
        for kind, source, held in inputs:
            take_all(held.at[part, pl.ds(0, others * rows)], in_recv.at[kind, part])
            own_copy(kind, part, held).wait()

    def wait_in_sent(part):
        for kind, source, held in inputs:
            take_all(turned.at[lax.rem(part, 2), kind, pl.ds(0, others)], in_send.at[kind, lax.rem(part, 2)])

    def fetch(part):
        copies = [
            pltpu.make_async_copy(held.at[part], buf, stage_sem.at[kind - 2])
            for kind, landed, held, buf, out in outputs
        ]
        for copy in copies:
            copy.start()
        for copy in copies:
            copy.wait()

    def store(part):
        copies = []
        for kind, landed, held, buf, out in outputs:
            copies.append(pltpu.make_async_copy(buf, held.at[part], stage_sem.at[kind - 2]))
            copies.append(
                pltpu.make_async_copy(buf.at[own_rows(me)], landed.at[part * peers + me], stage_sem.at[kind])
            )
        for copy in copies:
            copy.start()
        for copy in copies:
            copy.wait()

    def send_out(part):
        def one(who):
            for kind, landed, held, buf, out in outputs:
                remote(
                    held.at[part, own_rows(who)], landed.at[part * peers + me],
                    out_send.at[kind - 2], out_recv.at[kind - 2, part], who,
                ).start()

        each_peer(one)

    def send_last():
        for chunk in range(chunks):
            for kind, landed, held, buf, out in outputs:
                each_peer(
                    lambda who: remote(
                        held.at[last, some_rows(who, chunk)],
                        turned.at[spare, kind - 2, me, pl.ds(chunk * piece, piece)],
                        out_send.at[kind - 2], last_recv.at[kind - 2, chunk], who,
                    ).start()
                )

    def turn_out(part):
        for kind, landed, held, buf, out in outputs:
            take_all(landed.at[pl.ds(part * peers, others)], out_recv.at[kind - 2, part])
            copy = pltpu.make_async_copy(landed.at[pl.ds(part * peers, peers)], facing, stage_sem.at[0])
            copy.start()
            copy.wait()

            @pl.loop(0, rows // 16)
            def _(step):
                here = pl.ds(pl.multiple_of(step * 16, 16), 16)
                out[here, part * peers:(part + 1) * peers, :] = jnp.swapaxes(facing[:, here, :], 0, 1)

    def keep_own():
        for kind, landed, held, buf, out in outputs:
            turned[spare, kind - 2, me] = buf[own_rows(me), :]

    def turn_last():
        for chunk in range(chunks):
            for kind, landed, held, buf, out in outputs:
                take_all(
                    turned.at[spare, kind - 2, pl.ds(0, others), pl.ds(chunk * piece, piece)],
                    last_recv.at[kind - 2, chunk],
                )

                @pl.loop(chunk * (piece // 16), (chunk + 1) * (piece // 16))
                def _(step):
                    here = pl.ds(pl.multiple_of(step * 16, 16), 16)
                    out[here, last * peers:parts * peers, :] = jnp.swapaxes(
                        turned[spare, kind - 2, :, here, :], 0, 1
                    )

    def wait_out_sent():
        for kind, landed, held, buf, out in outputs:
            take_all(held.at[:, pl.ds(0, others * rows)], out_send.at[kind - 2])

    def at(step):
        return pl.ds(pl.multiple_of(step * tile, tile), tile)

    def dot(a, b, dims):
        return lax.dot_general(a, b, (dims, ((), ())), preferred_element_type=jnp.float32)

    def compute():
        @pl.loop(0, order // tile)
        def _(step):
            x = xbuf[at(step), :]
            zbuf[at(step), :] = dot(x, right[...], ((1,), (1,))).astype(jnp.bfloat16)
            sig = x.astype(jnp.float32)
            swish = sig * jax.nn.sigmoid(sig)
            cot = cbuf[at(step), :].astype(jnp.float32)
            dybuf[at(step), :] = (cot * swish).astype(jnp.bfloat16)

        @pl.loop(0, order // tile)
        def _(step):
            dzbuf[at(step), :] = dot(left[:, at(step)], dybuf[...], ((0,), (0,))).astype(jnp.bfloat16)
            grad_l[at(step), :] += dot(dybuf[at(step), :], zbuf[...], ((1,), (1,)))

        @pl.loop(0, width // tile)
        def _(step):
            grad_r[at(step), :] += dot(dzbuf[:, at(step)], xbuf[...], ((0,), (0,)))

        @pl.loop(0, order // tile)
        def _(step):
            y = dot(left[at(step), :], zbuf[...], ((1,), (0,))).astype(jnp.bfloat16).astype(jnp.float32)
            back = dot(dzbuf[at(step), :], right[...], ((1,), (0,)))
            sig = xbuf[at(step), :].astype(jnp.float32)
            cot = cbuf[at(step), :].astype(jnp.float32)
            gate = jax.nn.sigmoid(sig)
            xbuf[at(step), :] = (sig + y * (sig * gate)).astype(jnp.bfloat16)
            dswish = gate * (1.0 + sig * (1.0 - gate))
            cbuf[at(step), :] = (cot * (1.0 + y * dswish) + back).astype(jnp.bfloat16)

    def apply_mask(blocks, target):
        side = target.shape[0] // blocks.shape[0]

        @pl.loop(0, blocks.shape[0])
        def _(down):
            here = pl.ds(pl.multiple_of(down * side, side), side)
            for right_of in range(blocks.shape[1]):
                there = slice(right_of * side, (right_of + 1) * side)
                keep = blocks[down, right_of].astype(jnp.float32)
                target[here, there] = (target[here, there].astype(jnp.float32) * keep).astype(jnp.bfloat16)

    half = peers // 2
    parity = lax.rem(me, 2)
    chip = me // 2
    sibling = me + 1 - 2 * parity
    cols = width // groups
    grads = ((0, grad_r, right_blocks), (1, grad_l, left_blocks))

    def own_cols(line):
        return pl.ds(pl.multiple_of(line * cols, cols), cols)

    def start_pairs():
        @pl.loop(0, half)
        def _(block):
            for kind, grad, blocks in grads:
                remote(
                    grad.at[own_rows(2 * block + 1 - parity)], pairs.at[kind, block],
                    pair_sems.at[0, kind], pair_sems.at[1, kind], sibling,
                ).start()

    def send_along():
        for kind, grad, blocks in grads:
            take_all(pairs.at[kind], pair_sems.at[1, kind])

            @pl.loop(0, half)
            def _(block):
                total = grad[own_rows(2 * block + parity), :] + pairs[kind, block]
                grad[own_rows(2 * block + parity), :] = total
                zbuf[own_rows(kind * half + block), :] = total.astype(jnp.bfloat16)

            @pl.loop(1, groups)
            def _(step):
                other = lax.rem(column + step, groups)
                pltpu.make_async_remote_copy(
                    src_ref=zbuf.at[pl.ds(kind * half * rows, half * rows), own_cols(other)],
                    dst_ref=along.at[kind, column],
                    send_sem=along_sems.at[0, kind],
                    recv_sem=along_sems.at[1, kind],
                    device_id=(me, other),
                    device_id_type=pl.DeviceIdType.MESH,
                ).start()

    def partner(step):
        who = chip
        for bit in (1 << place for place in range(half.bit_length() - 1)):
            if step & bit:
                who = who + bit * (1 - 2 * lax.rem(chip // bit, 2))
        return who

    def sum_copies():
        copies = [pltpu.make_async_copy(own_sum, kept, sum_sem.at[0])]
        for step in range(1, half):
            copies.append(
                pltpu.make_async_copy(
                    summed.at[:, partner(step)], away[step - 1], sum_sem.at[step]
                )
            )
        return copies

    def sum_along():
        for kind, grad, blocks in grads:
            take_all(along.at[kind, pl.ds(0, groups - 1)], along_sems.at[1, kind])
            side = width // blocks.shape[0]

            @pl.loop(0, half)
            def _(block):
                whose = 2 * block + parity
                total = grad[own_rows(whose), own_cols(column)]
                for step in range(1, groups):
                    other = lax.rem(column + step, groups)
                    total = total + along[kind, other, own_rows(block), :].astype(jnp.float32)
                for right_of in range(cols // side):
                    there = slice(right_of * side, (right_of + 1) * side)
                    keep = blocks[whose * rows // side, column * (cols // side) + right_of].astype(jnp.float32)
                    term = total[:, there] * keep / scales[kind]
                    summed[kind, block, :, there] = term.astype(jnp.bfloat16)

                    @pl.when(block == chip)
                    def _():
                        own_sum[kind, :, there] = term

        for copy in sum_copies():
            copy.start()

    def wait_sums():
        for kind, grad, blocks in grads:
            take_all(pairs.at[kind], pair_sems.at[0, kind])
            take_all(along.at[kind, pl.ds(0, groups - 1)], along_sems.at[0, kind])
        for copy in sum_copies():
            copy.wait()

    def tell_free():
        def one(who):
            pl.semaphore_signal(
                free_sem, inc=1, device_id=(who, column), device_id_type=pl.DeviceIdType.MESH
            )

        each_peer(one)

    fetched = (
        pltpu.make_async_copy(right_in, right, load_sem.at[2]),
        pltpu.make_async_copy(left_in, left, load_sem.at[3]),
    )
    send_first()
    if parts > 1:
        load(1, 0, signal).start()
    for copy in fetched:
        copy.start()
    if parts > 1:
        send_in(1)
    if parts > 2:
        load(2, 0, signal).start()
    for copy in fetched:
        copy.wait()
    grad_r[...] = jnp.zeros_like(grad_r)
    grad_l[...] = jnp.zeros_like(grad_l)
    apply_mask(right_blocks, right)
    apply_mask(left_blocks, left)

    @pl.loop(0, parts)
    def _(part):
        wait_in(part)

        @pl.when(part + 2 < parts)
        def _():
            wait_in_sent(part)
            send_in(part + 2)

        @pl.when(part + 3 < parts)
        def _():
            load(part + 3, 0, signal).start()

        @pl.when(part == last)
        def _():
            if parts > 1:
                wait_in_sent(last - 1)
            tell_free()

        fetch(part)
        compute()

        @pl.when(part == last)
        def _():
            start_pairs()

        store(part)

        @pl.when(part < last)
        def _():
            send_out(part)

    pl.semaphore_wait(free_sem, others)
    send_last()
    keep_own()
    send_along()
    if last > 0:
        turn_out(0)
    sum_along()
    for part in range(1, last):
        turn_out(part)
    wait_in_sent(last)
    wait_sums()
    turn_last()
    wait_out_sent()


def hand_over(mixed, grad, out_m, out_g, sems):
    copies = (
        pltpu.make_async_copy(mixed, out_m, sems.at[0]),
        pltpu.make_async_copy(grad, out_g, sems.at[1]),
    )
    for copy in copies:
        copy.start()
    for copy in copies:
        copy.wait()


def shards_by_channel(signal, cotangent, right_factor, left_factor, right_blocks, left_blocks):
    rows_here, chans, width_two = signal.shape
    width_one = left_factor.shape[0]
    peers = lax.axis_size("seq")
    groups = lax.axis_size("ch")
    parts = chans // peers
    half = peers // 2
    cols = width_two // groups
    chunks = 4
    square = (width_one, width_two)
    scales = (math.sqrt(width_one * chans * groups), math.sqrt(width_two * chans * groups))
    hbm = pl.BlockSpec(memory_space=pl.ANY)
    vmem = pl.BlockSpec(memory_space=pltpu.VMEM)
    smem = pl.BlockSpec(memory_space=pltpu.SMEM)
    result = jax.ShapeDtypeStruct(signal.shape, jnp.bfloat16)
    held = jax.ShapeDtypeStruct((parts, *square), jnp.bfloat16)
    landed = jax.ShapeDtypeStruct((chans, rows_here, width_two), jnp.bfloat16)
    kept = jax.ShapeDtypeStruct((2, rows_here, cols), jnp.float32)
    away = jax.ShapeDtypeStruct((2, rows_here, cols), jnp.bfloat16)
    mixed, grad, _, _, _, _, total, *terms = pl.pallas_call(
        functools.partial(mix_kernel, peers, groups, parts, chunks, scales),
        out_shape=(pltpu.VMEM(signal.shape, jnp.bfloat16),) * 2
        + (held, held, landed, landed, kept)
        + (away,) * (half - 1),
        in_specs=[smem, smem, hbm, hbm, hbm, hbm],
        out_specs=(vmem,) * 2 + (hbm,) * (4 + half),
        scratch_shapes=[
            pltpu.VMEM(square, jnp.bfloat16),
            pltpu.VMEM(square, jnp.bfloat16),
            pltpu.VMEM(square, jnp.float32),
            pltpu.VMEM(square, jnp.float32),
            pltpu.VMEM(square, jnp.bfloat16),
            pltpu.VMEM(square, jnp.bfloat16),
            pltpu.VMEM(square, jnp.bfloat16),
            pltpu.VMEM(square, jnp.bfloat16),
            pltpu.VMEM(square, jnp.bfloat16),
            pltpu.VMEM((2, half, rows_here, width_two), jnp.float32),
            pltpu.VMEM((2, groups, half * rows_here, cols), jnp.bfloat16),
            pltpu.VMEM((2, half, rows_here, cols), jnp.bfloat16),
            pltpu.VMEM((2, rows_here, cols), jnp.float32),
            pltpu.VMEM((rows_here, peers, width_two), jnp.bfloat16),
            pltpu.VMEM((peers, rows_here, width_two), jnp.bfloat16),
            pltpu.VMEM((2, 2, peers, rows_here, width_two), jnp.bfloat16),
            pltpu.SemaphoreType.DMA((2, 2)),
            pltpu.SemaphoreType.DMA((2, parts)),
            pltpu.SemaphoreType.DMA((2, 2)),
            pltpu.SemaphoreType.DMA((2,)),
            pltpu.SemaphoreType.DMA((2, parts)),
            pltpu.SemaphoreType.DMA((2, chunks)),
            pltpu.SemaphoreType.DMA((4,)),
            pltpu.SemaphoreType.DMA((2, 2)),
            pltpu.SemaphoreType.DMA((2, 2)),
            pltpu.SemaphoreType.DMA((half,)),
            pltpu.SemaphoreType.DMA((4,)),
            pltpu.SemaphoreType.DMA((chunks,)),
            pltpu.SemaphoreType.REGULAR,
        ],
        compiler_params=pltpu.CompilerParams(
            collective_id=0, has_side_effects=True, vmem_limit_bytes=47 * 2**20
        ),
    )(right_blocks, left_blocks, signal, cotangent, right_factor, left_factor)
    for step, term in enumerate(terms, 1):
        pairs = [(who, who ^ (2 * step)) for who in range(peers)]
        total = total + lax.ppermute(term, "seq", pairs).astype(jnp.float32)
    mixed, grad = (pltpu.with_memory_space_constraint(array, pltpu.VMEM) for array in (mixed, grad))
    mixed, grad = pl.pallas_call(
        hand_over,
        out_shape=(result, result),
        in_specs=[vmem, vmem],
        out_specs=(hbm, hbm),
        scratch_shapes=[pltpu.SemaphoreType.DMA((2,))],
        compiler_params=pltpu.CompilerParams(vmem_limit_bytes=2**20),
        cost_estimate=pl.CostEstimate(flops=0, bytes_accessed=4 * signal.size, transcendentals=0),
    )(mixed, grad)
    return (mixed, grad, total[0], total[1])


def shards(signal, *others):
    rows_here, chans, width_two = signal.shape
    peers = lax.axis_size("seq")
    width_one = others[1].shape[0]
    sides = (width_two // others[3].shape[0], width_one // others[4].shape[0])
    fits = chans % peers == 0 and rows_here % 16 == 0 and peers & (peers - 1) == 0
    fits = fits and sides == (128, 128) and rows_here == 128
    fits = fits and width_two // lax.axis_size("ch") % 128 == 0
    if fits and width_one == 1024 and width_two == 1024 and chans // peers <= 4:
        return shards_by_channel(signal, *others)
    return shards_by_column(signal, *others)


def solution(mesh):
    return jax.shard_map(
        shards,
        mesh=mesh,
        in_specs=(P("seq", "ch", None), P("seq", "ch", None), P(), P(), P(), P()),
        out_specs=(P("seq", "ch", None), P("seq", "ch", None), P("seq", "ch"), P("seq", "ch")),
        check_vma=False,
    )
```

```python
import functools
import math

import jax
import jax.numpy as jnp
from jax import lax
from jax.experimental import pallas as pl
from jax.experimental.pallas import tpu as pltpu
from jax.sharding import PartitionSpec as P


def expand(blocks, width):
    tile = width // blocks.shape[0]
    return jnp.repeat(jnp.repeat(blocks, tile, axis=0), tile, axis=1)


def to_columns(rows, peers):
    rows_here, chans, width_two = rows.shape
    piece = width_two // peers
    arranged = rows.reshape(rows_here, chans, peers, piece).transpose(0, 2, 1, 3)
    return arranged.reshape(rows_here, peers, chans * piece)


def to_rows(received, chans):
    rows_here, peers, wide = received.shape
    piece = wide // chans
    arranged = received.reshape(rows_here, peers, chans, piece).transpose(0, 2, 1, 3)
    return arranged.reshape(rows_here, chans, peers * piece)


def shards_by_column(signal, cotangent, right_factor, left_factor, right_blocks, left_blocks):
    rows_here, chans, width_two = signal.shape
    width_one = left_factor.shape[0]
    peers = lax.axis_size("seq")
    right_mask = expand(right_blocks, width_two).astype(jnp.bfloat16)
    left_mask = expand(left_blocks, width_one).astype(jnp.bfloat16)
    right_eff = right_factor * right_mask
    left_eff = left_factor * left_mask
    flat_signal = signal.reshape(rows_here * chans, width_two)
    first_rows = jnp.dot(flat_signal, right_eff.T, preferred_element_type=jnp.float32)
    first_rows = to_columns(
        first_rows.astype(jnp.bfloat16).reshape(rows_here, chans, width_two), peers
    )
    sig_f = signal.astype(jnp.float32)
    gate = jax.nn.sigmoid(sig_f)
    swish = sig_f * gate
    cot_f = cotangent.astype(jnp.float32)
    grad_rows = to_columns((cot_f * swish).astype(jnp.bfloat16), peers)
    z_cols = lax.all_to_all(first_rows, "seq", split_axis=1, concat_axis=0, tiled=True)
    flat_cols = z_cols.reshape(width_one, z_cols.shape[2])
    result = jnp.dot(left_eff, flat_cols, preferred_element_type=jnp.float32)
    y_cols = result.astype(jnp.bfloat16).reshape(width_one, 1, z_cols.shape[2])
    y_back = lax.all_to_all(y_cols, "seq", split_axis=0, concat_axis=1, tiled=True)
    dy_cols = lax.all_to_all(grad_rows, "seq", split_axis=1, concat_axis=0, tiled=True)
    flat_cols = dy_cols.reshape(width_one, dy_cols.shape[2])
    result = lax.dot_general(
        left_eff, flat_cols, (((0,), (0,)), ((), ())), preferred_element_type=jnp.float32
    )
    dz_cols = result.astype(jnp.bfloat16).reshape(width_one, 1, dy_cols.shape[2])
    dz_back = lax.all_to_all(dz_cols, "seq", split_axis=0, concat_axis=1, tiled=True)
    y_rows = to_rows(y_back, chans)
    dz_rows = to_rows(dz_back, chans)
    y_f = y_rows.astype(jnp.float32)
    mixed = (sig_f + y_f * swish).astype(jnp.bfloat16)
    dz_flat = dz_rows.reshape(rows_here * chans, width_two)
    back = jnp.dot(dz_flat, right_eff, preferred_element_type=jnp.float32).reshape(
        rows_here, chans, width_two
    )
    dswish = gate * (1.0 + sig_f * (1.0 - gate))
    grad_signal = (cot_f * (1.0 + y_f * dswish) + back).astype(jnp.bfloat16)
    wide = z_cols.shape[2]
    z_flat = z_cols.reshape(width_one, wide)
    dy_flat = dy_cols.reshape(width_one, wide)
    left_term = lax.dot_general(
        dy_flat, z_flat, (((1,), (1,)), ((), ())), preferred_element_type=jnp.float32
    )
    right_term = lax.dot_general(
        dz_flat, flat_signal, (((0,), (0,)), ((), ())), preferred_element_type=jnp.float32
    )
    total_chans = chans * lax.axis_size("ch")
    right_term = right_term * right_mask.astype(jnp.float32) / math.sqrt(width_one * total_chans)
    left_term = left_term * left_mask.astype(jnp.float32) / math.sqrt(width_two * total_chans)
    partial_value = (
        lax.psum_scatter(right_term, "seq", scatter_dimension=0, tiled=True),
        lax.psum_scatter(left_term, "seq", scatter_dimension=0, tiled=True),
    )
    grad_right, grad_left = (
        lax.psum_scatter(partial_value[0], "ch", scatter_dimension=1, tiled=True),
        lax.psum_scatter(partial_value[1], "ch", scatter_dimension=1, tiled=True),
    )
    return (mixed, grad_signal, grad_right, grad_left)


def mix_kernel(peers, groups, parts, chunks, scales, *refs):
    right_blocks, left_blocks, signal, cotangent, right_in, left_in, *refs = refs
    out_m, out_g, xh, ch, mt, gt, kept, *refs = refs
    away, refs = refs[:peers // 2 - 1], refs[peers // 2 - 1:]
    right, left, grad_r, grad_l, xbuf, cbuf, zbuf, dybuf, dzbuf, *refs = refs
    pairs, along, summed, own_sum, slab, facing, turned, *refs = refs
    in_send, in_recv, own_in_sem, out_send, out_recv, last_recv, stage_sem, *refs = refs
    pair_sems, along_sems, sum_sem, load_sem, first_sem, free_sem, line_sem, all_sem = refs
    me = lax.axis_index("seq")
    column = lax.axis_index("ch")
    rows = signal.shape[0]
    width = signal.shape[2]
    order = left.shape[0]
    tile = 256
    piece = rows // chunks
    last = parts - 1
    others = peers - 1
    spare = parts % 2

    def own_rows(who):
        return pl.ds(pl.multiple_of(who * rows, rows), rows)

    def some_rows(who, chunk):
        return pl.ds(pl.multiple_of(who * rows + chunk * piece, piece), piece)

    def remote(source, target, going, coming, who):
        return pltpu.make_async_remote_copy(
            src_ref=source,
            dst_ref=target,
            send_sem=going,
            recv_sem=coming,
            device_id=(who, column),
            device_id_type=pl.DeviceIdType.MESH,
        )

    def take_all(ref, sem):
        pltpu.make_async_copy(ref, ref, sem).wait()

    def each_peer(action):
        @pl.loop(1, peers)
        def _(step):
            action(lax.rem(me + step, peers))

    barrier = pltpu.get_barrier_semaphore()

    def load(part, kind, source):
        there = pl.ds(pl.multiple_of(part * peers, peers), peers)
        return pltpu.make_async_copy(source.at[:, there, :], slab, load_sem.at[kind])

    def first_load(chunk):
        here = pl.ds(chunk * piece, piece)
        return pltpu.make_async_copy(signal.at[here, pl.ds(0, peers), :], slab.at[here], first_sem.at[chunk])

    for chunk in range(chunks):
        first_load(chunk).start()

    def tell(sem, who, line):
        pl.semaphore_signal(sem, inc=1, device_id=(who, line), device_id_type=pl.DeviceIdType.MESH)

    def tell_line(sem):
        @pl.loop(1, groups)
        def _(step):
            tell(sem, me, lax.rem(column + step, groups))

    gate = me == 0
    greeted = others + (groups - 1) * ((others - me) // others)

    @pl.when(gate)
    def _():
        tell_line(barrier)

    each_peer(lambda who: tell(barrier, who, column))

    inputs = ((0, signal, xh), (1, cotangent, ch))
    outputs = ((2, mt, xh, xbuf, out_m), (3, gt, ch, cbuf, out_g))

    def turn(part, kind, chunk, count):
        @pl.loop(chunk * (piece // 16), (chunk + count) * (piece // 16))
        def _(step):
            here = pl.ds(pl.multiple_of(step * 16, 16), 16)
            turned[lax.rem(part, 2), kind, :, here, :] = jnp.swapaxes(slab[here], 0, 1)

    def in_copy(kind, part, held, who, at_rows, there):
        return remote(
            turned.at[lax.rem(part, 2), kind, who, at_rows],
            held.at[part, there],
            in_send.at[kind, lax.rem(part, 2)],
            in_recv.at[kind, part],
            who,
        )

    def whole_in_copy(kind, part, held, who):
        return in_copy(kind, part, held, who, pl.ds(0, rows), own_rows(me))

    def own_copy(kind, part, held):
        return pltpu.make_async_copy(
            turned.at[lax.rem(part, 2), kind, me], held.at[part, own_rows(me)], own_in_sem.at[kind, lax.rem(part, 2)]
        )

    def send_in(part):
        for kind, source, held in inputs:
            load(part, kind, source).wait()
            turn(part, kind, 0, chunks)
            if kind == 0:
                load(part, 1, cotangent).start()
            each_peer(lambda who: whole_in_copy(kind, part, held, who).start())
            own_copy(kind, part, held).start()

    def send_first():
        for kind, source, held in inputs:
            if kind == 1:
                load(0, kind, source).wait()
            for chunk in range(chunks):
                if kind == 0:
                    first_load(chunk).wait()
                turn(0, kind, chunk, 1)
                if kind == 0 and chunk == 0:
                    pl.semaphore_wait(barrier, greeted)
                each_peer(
                    lambda who: in_copy(
                        kind, 0, held, who, pl.ds(chunk * piece, piece), some_rows(me, chunk)
                    ).start()
                )
            if kind == 0:
                load(0, 1, cotangent).start()
            own_copy(kind, 0, held).start()

    def wait_in(part):
        for kind, source, held in inputs:
            take_all(held.at[part, pl.ds(0, others * rows)], in_recv.at[kind, part])
            own_copy(kind, part, held).wait()

    def wait_in_sent(part):
        for kind, source, held in inputs:
            take_all(turned.at[lax.rem(part, 2), kind, pl.ds(0, others)], in_send.at[kind, lax.rem(part, 2)])

    def fetch(part):
        copies = [
            pltpu.make_async_copy(held.at[part], buf, stage_sem.at[kind - 2])
            for kind, landed, held, buf, out in outputs
        ]
        for copy in copies:
            copy.start()
        for copy in copies:
            copy.wait()

    def store(part):
        copies = []
        for kind, landed, held, buf, out in outputs:
            copies.append(pltpu.make_async_copy(buf, held.at[part], stage_sem.at[kind - 2]))
            copies.append(
                pltpu.make_async_copy(buf.at[own_rows(me)], landed.at[part * peers + me], stage_sem.at[kind])
            )
        for copy in copies:
            copy.start()
        for copy in copies:
            copy.wait()

    def send_out(part):
        def one(who):
            for kind, landed, held, buf, out in outputs:
                remote(
                    held.at[part, own_rows(who)], landed.at[part * peers + me],
                    out_send.at[kind - 2], out_recv.at[kind - 2, part], who,
                ).start()

        each_peer(one)

    def send_last():
        for chunk in range(chunks):
            for kind, landed, held, buf, out in outputs:
                each_peer(
                    lambda who: remote(
                        held.at[last, some_rows(who, chunk)],
                        turned.at[spare, kind - 2, me, pl.ds(chunk * piece, piece)],
                        out_send.at[kind - 2], last_recv.at[kind - 2, chunk], who,
                    ).start()
                )

    def turn_out(part):
        for kind, landed, held, buf, out in outputs:
            take_all(landed.at[pl.ds(part * peers, others)], out_recv.at[kind - 2, part])
            copy = pltpu.make_async_copy(landed.at[pl.ds(part * peers, peers)], facing, stage_sem.at[0])
            copy.start()
            copy.wait()

            @pl.loop(0, rows // 16)
            def _(step):
                here = pl.ds(pl.multiple_of(step * 16, 16), 16)
                out[here, part * peers:(part + 1) * peers, :] = jnp.swapaxes(facing[:, here, :], 0, 1)

    def keep_own():
        for kind, landed, held, buf, out in outputs:
            turned[spare, kind - 2, me] = buf[own_rows(me), :]

    def turn_last():
        for chunk in range(chunks):
            for kind, landed, held, buf, out in outputs:
                take_all(
                    turned.at[spare, kind - 2, pl.ds(0, others), pl.ds(chunk * piece, piece)],
                    last_recv.at[kind - 2, chunk],
                )

                @pl.loop(chunk * (piece // 16), (chunk + 1) * (piece // 16))
                def _(step):
                    here = pl.ds(pl.multiple_of(step * 16, 16), 16)
                    out[here, last * peers:parts * peers, :] = jnp.swapaxes(
                        turned[spare, kind - 2, :, here, :], 0, 1
                    )

    def wait_out_sent():
        for kind, landed, held, buf, out in outputs:
            take_all(held.at[:, pl.ds(0, others * rows)], out_send.at[kind - 2])

    def at(step):
        return pl.ds(pl.multiple_of(step * tile, tile), tile)

    def dot(a, b, dims):
        return lax.dot_general(a, b, (dims, ((), ())), preferred_element_type=jnp.float32)

    def compute():
        @pl.loop(0, order // tile)
        def _(step):
            x = xbuf[at(step), :]
            zbuf[at(step), :] = dot(x, right[...], ((1,), (1,))).astype(jnp.bfloat16)
            sig = x.astype(jnp.float32)
            swish = sig * jax.nn.sigmoid(sig)
            cot = cbuf[at(step), :].astype(jnp.float32)
            dybuf[at(step), :] = (cot * swish).astype(jnp.bfloat16)

        @pl.loop(0, order // tile)
        def _(step):
            dzbuf[at(step), :] = dot(left[:, at(step)], dybuf[...], ((0,), (0,))).astype(jnp.bfloat16)
            grad_l[at(step), :] += dot(dybuf[at(step), :], zbuf[...], ((1,), (1,)))

        @pl.loop(0, width // tile)
        def _(step):
            grad_r[at(step), :] += dot(dzbuf[:, at(step)], xbuf[...], ((0,), (0,)))

        @pl.loop(0, order // tile)
        def _(step):
            y = dot(left[at(step), :], zbuf[...], ((1,), (0,))).astype(jnp.bfloat16).astype(jnp.float32)
            back = dot(dzbuf[at(step), :], right[...], ((1,), (0,)))
            sig = xbuf[at(step), :].astype(jnp.float32)
            cot = cbuf[at(step), :].astype(jnp.float32)
            gate = jax.nn.sigmoid(sig)
            xbuf[at(step), :] = (sig + y * (sig * gate)).astype(jnp.bfloat16)
            dswish = gate * (1.0 + sig * (1.0 - gate))
            cbuf[at(step), :] = (cot * (1.0 + y * dswish) + back).astype(jnp.bfloat16)

    def apply_mask(blocks, target):
        side = target.shape[0] // blocks.shape[0]

        @pl.loop(0, blocks.shape[0])
        def _(down):
            here = pl.ds(pl.multiple_of(down * side, side), side)
            for right_of in range(blocks.shape[1]):
                there = slice(right_of * side, (right_of + 1) * side)
                keep = blocks[down, right_of].astype(jnp.float32)
                target[here, there] = (target[here, there].astype(jnp.float32) * keep).astype(jnp.bfloat16)

    half = peers // 2
    parity = lax.rem(me, 2)
    chip = me // 2
    sibling = me + 1 - 2 * parity
    cols = width // groups
    grads = ((0, grad_r, right_blocks), (1, grad_l, left_blocks))

    def own_cols(line):
        return pl.ds(pl.multiple_of(line * cols, cols), cols)

    def start_pairs():
        @pl.loop(0, half)
        def _(block):
            for kind, grad, blocks in grads:
                remote(
                    grad.at[own_rows(2 * block + 1 - parity)], pairs.at[kind, block],
                    pair_sems.at[0, kind], pair_sems.at[1, kind], sibling,
                ).start()

    def send_along():
        for kind, grad, blocks in grads:
            take_all(pairs.at[kind], pair_sems.at[1, kind])

            @pl.loop(0, half)
            def _(block):
                total = grad[own_rows(2 * block + parity), :] + pairs[kind, block]
                grad[own_rows(2 * block + parity), :] = total
                zbuf[own_rows(kind * half + block), :] = total.astype(jnp.bfloat16)

            @pl.loop(1, groups)
            def _(step):
                other = lax.rem(column + step, groups)
                pltpu.make_async_remote_copy(
                    src_ref=zbuf.at[pl.ds(kind * half * rows, half * rows), own_cols(other)],
                    dst_ref=along.at[kind, column],
                    send_sem=along_sems.at[0, kind],
                    recv_sem=along_sems.at[1, kind],
                    device_id=(me, other),
                    device_id_type=pl.DeviceIdType.MESH,
                ).start()

    def partner(step):
        who = chip
        for bit in (1 << place for place in range(half.bit_length() - 1)):
            if step & bit:
                who = who + bit * (1 - 2 * lax.rem(chip // bit, 2))
        return who

    def sum_copies():
        copies = [pltpu.make_async_copy(own_sum, kept, sum_sem.at[0])]
        for step in range(1, half):
            copies.append(
                pltpu.make_async_copy(
                    summed.at[:, partner(step)], away[step - 1], sum_sem.at[step]
                )
            )
        return copies

    def sum_along():
        for kind, grad, blocks in grads:
            take_all(along.at[kind, pl.ds(0, groups - 1)], along_sems.at[1, kind])
            side = width // blocks.shape[0]

            @pl.loop(0, half)
            def _(block):
                whose = 2 * block + parity
                total = grad[own_rows(whose), own_cols(column)]
                for step in range(1, groups):
                    other = lax.rem(column + step, groups)
                    total = total + along[kind, other, own_rows(block), :].astype(jnp.float32)
                for right_of in range(cols // side):
                    there = slice(right_of * side, (right_of + 1) * side)
                    keep = blocks[whose * rows // side, column * (cols // side) + right_of].astype(jnp.float32)
                    term = total[:, there] * keep / scales[kind]
                    summed[kind, block, :, there] = term.astype(jnp.bfloat16)

                    @pl.when(block == chip)
                    def _():
                        own_sum[kind, :, there] = term

        for copy in sum_copies():
            copy.start()

    def wait_sums():
        for kind, grad, blocks in grads:
            take_all(pairs.at[kind], pair_sems.at[0, kind])
            take_all(along.at[kind, pl.ds(0, groups - 1)], along_sems.at[0, kind])
        for copy in sum_copies():
            copy.wait()

    fetched = (
        pltpu.make_async_copy(right_in, right, load_sem.at[2]),
        pltpu.make_async_copy(left_in, left, load_sem.at[3]),
    )
    send_first()
    if parts > 1:
        load(1, 0, signal).start()
    for copy in fetched:
        copy.start()

    @pl.when(gate)
    def _():
        tell_line(line_sem)

    if parts > 1:
        send_in(1)
    if parts > 2:
        load(2, 0, signal).start()
    for copy in fetched:
        copy.wait()
    grad_r[...] = jnp.zeros_like(grad_r)
    grad_l[...] = jnp.zeros_like(grad_l)
    apply_mask(right_blocks, right)
    apply_mask(left_blocks, left)

    @pl.when(gate)
    def _():
        pl.semaphore_wait(line_sem, groups - 1)
        each_peer(lambda who: tell(all_sem, who, column))

    @pl.loop(0, parts)
    def _(part):
        wait_in(part)

        @pl.when(part + 2 < parts)
        def _():
            wait_in_sent(part)
            send_in(part + 2)

        @pl.when(part + 3 < parts)
        def _():
            load(part + 3, 0, signal).start()

        @pl.when(part == last)
        def _():
            if parts > 1:
                wait_in_sent(last - 1)
            each_peer(lambda who: tell(free_sem, who, column))

        fetch(part)
        compute()

        @pl.when(part == last)
        def _():
            start_pairs()

        store(part)

        @pl.when(part < last)
        def _():
            send_out(part)

    pl.semaphore_wait(free_sem, others)
    send_last()
    keep_own()

    @pl.when(me > 0)
    def _():
        pl.semaphore_wait(all_sem, 1)

    send_along()
    if last > 0:
        turn_out(0)
    sum_along()
    for part in range(1, last):
        turn_out(part)
    wait_in_sent(last)
    wait_sums()
    turn_last()
    wait_out_sent()


def hand_over(mixed, grad, out_m, out_g, sems):
    copies = (
        pltpu.make_async_copy(mixed, out_m, sems.at[0]),
        pltpu.make_async_copy(grad, out_g, sems.at[1]),
    )
    for copy in copies:
        copy.start()
    for copy in copies:
        copy.wait()


def shards_by_channel(signal, cotangent, right_factor, left_factor, right_blocks, left_blocks):
    rows_here, chans, width_two = signal.shape
    width_one = left_factor.shape[0]
    peers = lax.axis_size("seq")
    groups = lax.axis_size("ch")
    parts = chans // peers
    half = peers // 2
    cols = width_two // groups
    chunks = 4
    square = (width_one, width_two)
    scales = (math.sqrt(width_one * chans * groups), math.sqrt(width_two * chans * groups))
    hbm = pl.BlockSpec(memory_space=pl.ANY)
    vmem = pl.BlockSpec(memory_space=pltpu.VMEM)
    smem = pl.BlockSpec(memory_space=pltpu.SMEM)
    result = jax.ShapeDtypeStruct(signal.shape, jnp.bfloat16)
    held = jax.ShapeDtypeStruct((parts, *square), jnp.bfloat16)
    landed = jax.ShapeDtypeStruct((chans, rows_here, width_two), jnp.bfloat16)
    kept = jax.ShapeDtypeStruct((2, rows_here, cols), jnp.float32)
    away = jax.ShapeDtypeStruct((2, rows_here, cols), jnp.bfloat16)
    mixed, grad, _, _, _, _, total, *terms = pl.pallas_call(
        functools.partial(mix_kernel, peers, groups, parts, chunks, scales),
        out_shape=(pltpu.VMEM(signal.shape, jnp.bfloat16),) * 2
        + (held, held, landed, landed, kept)
        + (away,) * (half - 1),
        in_specs=[smem, smem, hbm, hbm, hbm, hbm],
        out_specs=(vmem,) * 2 + (hbm,) * (4 + half),
        scratch_shapes=[
            pltpu.VMEM(square, jnp.bfloat16),
            pltpu.VMEM(square, jnp.bfloat16),
            pltpu.VMEM(square, jnp.float32),
            pltpu.VMEM(square, jnp.float32),
            pltpu.VMEM(square, jnp.bfloat16),
            pltpu.VMEM(square, jnp.bfloat16),
            pltpu.VMEM(square, jnp.bfloat16),
            pltpu.VMEM(square, jnp.bfloat16),
            pltpu.VMEM(square, jnp.bfloat16),
            pltpu.VMEM((2, half, rows_here, width_two), jnp.float32),
            pltpu.VMEM((2, groups, half * rows_here, cols), jnp.bfloat16),
            pltpu.VMEM((2, half, rows_here, cols), jnp.bfloat16),
            pltpu.VMEM((2, rows_here, cols), jnp.float32),
            pltpu.VMEM((rows_here, peers, width_two), jnp.bfloat16),
            pltpu.VMEM((peers, rows_here, width_two), jnp.bfloat16),
            pltpu.VMEM((2, 2, peers, rows_here, width_two), jnp.bfloat16),
            pltpu.SemaphoreType.DMA((2, 2)),
            pltpu.SemaphoreType.DMA((2, parts)),
            pltpu.SemaphoreType.DMA((2, 2)),
            pltpu.SemaphoreType.DMA((2,)),
            pltpu.SemaphoreType.DMA((2, parts)),
            pltpu.SemaphoreType.DMA((2, chunks)),
            pltpu.SemaphoreType.DMA((4,)),
            pltpu.SemaphoreType.DMA((2, 2)),
            pltpu.SemaphoreType.DMA((2, 2)),
            pltpu.SemaphoreType.DMA((half,)),
            pltpu.SemaphoreType.DMA((4,)),
            pltpu.SemaphoreType.DMA((chunks,)),
            pltpu.SemaphoreType.REGULAR,
            pltpu.SemaphoreType.REGULAR,
            pltpu.SemaphoreType.REGULAR,
        ],
        compiler_params=pltpu.CompilerParams(
            collective_id=0, has_side_effects=True, vmem_limit_bytes=47 * 2**20
        ),
    )(right_blocks, left_blocks, signal, cotangent, right_factor, left_factor)
    for step, term in enumerate(terms, 1):
        pairs = [(who, who ^ (2 * step)) for who in range(peers)]
        total = total + lax.ppermute(term, "seq", pairs).astype(jnp.float32)
    mixed, grad = (pltpu.with_memory_space_constraint(array, pltpu.VMEM) for array in (mixed, grad))
    mixed, grad = pl.pallas_call(
        hand_over,
        out_shape=(result, result),
        in_specs=[vmem, vmem],
        out_specs=(hbm, hbm),
        scratch_shapes=[pltpu.SemaphoreType.DMA((2,))],
        compiler_params=pltpu.CompilerParams(vmem_limit_bytes=2**20),
        cost_estimate=pl.CostEstimate(flops=0, bytes_accessed=4 * signal.size, transcendentals=0),
    )(mixed, grad)
    return (mixed, grad, total[0], total[1])


def shards(signal, *others):
    rows_here, chans, width_two = signal.shape
    peers = lax.axis_size("seq")
    width_one = others[1].shape[0]
    sides = (width_two // others[3].shape[0], width_one // others[4].shape[0])
    fits = chans % peers == 0 and rows_here % 16 == 0 and peers & (peers - 1) == 0
    fits = fits and sides == (128, 128) and rows_here == 128
    fits = fits and width_two // lax.axis_size("ch") % 128 == 0
    if fits and width_one == 1024 and width_two == 1024 and chans // peers <= 4:
        return shards_by_channel(signal, *others)
    return shards_by_column(signal, *others)


def solution(mesh):
    return jax.shard_map(
        shards,
        mesh=mesh,
        in_specs=(P("seq", "ch", None), P("seq", "ch", None), P(), P(), P(), P()),
        out_specs=(P("seq", "ch", None), P("seq", "ch", None), P("seq", "ch"), P("seq", "ch")),
        check_vma=False,
    )
```

```python
import functools
import math

import jax
import jax.numpy as jnp
from jax import lax
from jax.experimental import pallas as pl
from jax.experimental.pallas import tpu as pltpu
from jax.sharding import PartitionSpec as P


def expand(blocks, width):
    tile = width // blocks.shape[0]
    return jnp.repeat(jnp.repeat(blocks, tile, axis=0), tile, axis=1)


def to_columns(rows, peers):
    rows_here, chans, width_two = rows.shape
    piece = width_two // peers
    arranged = rows.reshape(rows_here, chans, peers, piece).transpose(0, 2, 1, 3)
    return arranged.reshape(rows_here, peers, chans * piece)


def to_rows(received, chans):
    rows_here, peers, wide = received.shape
    piece = wide // chans
    arranged = received.reshape(rows_here, peers, chans, piece).transpose(0, 2, 1, 3)
    return arranged.reshape(rows_here, chans, peers * piece)


def shards_by_column(signal, cotangent, right_factor, left_factor, right_blocks, left_blocks):
    rows_here, chans, width_two = signal.shape
    width_one = left_factor.shape[0]
    peers = lax.axis_size("seq")
    right_mask = expand(right_blocks, width_two).astype(jnp.bfloat16)
    left_mask = expand(left_blocks, width_one).astype(jnp.bfloat16)
    right_eff = right_factor * right_mask
    left_eff = left_factor * left_mask
    flat_signal = signal.reshape(rows_here * chans, width_two)
    first_rows = jnp.dot(flat_signal, right_eff.T, preferred_element_type=jnp.float32)
    first_rows = to_columns(
        first_rows.astype(jnp.bfloat16).reshape(rows_here, chans, width_two), peers
    )
    sig_f = signal.astype(jnp.float32)
    gate = jax.nn.sigmoid(sig_f)
    swish = sig_f * gate
    cot_f = cotangent.astype(jnp.float32)
    grad_rows = to_columns((cot_f * swish).astype(jnp.bfloat16), peers)
    z_cols = lax.all_to_all(first_rows, "seq", split_axis=1, concat_axis=0, tiled=True)
    flat_cols = z_cols.reshape(width_one, z_cols.shape[2])
    result = jnp.dot(left_eff, flat_cols, preferred_element_type=jnp.float32)
    y_cols = result.astype(jnp.bfloat16).reshape(width_one, 1, z_cols.shape[2])
    y_back = lax.all_to_all(y_cols, "seq", split_axis=0, concat_axis=1, tiled=True)
    dy_cols = lax.all_to_all(grad_rows, "seq", split_axis=1, concat_axis=0, tiled=True)
    flat_cols = dy_cols.reshape(width_one, dy_cols.shape[2])
    result = lax.dot_general(
        left_eff, flat_cols, (((0,), (0,)), ((), ())), preferred_element_type=jnp.float32
    )
    dz_cols = result.astype(jnp.bfloat16).reshape(width_one, 1, dy_cols.shape[2])
    dz_back = lax.all_to_all(dz_cols, "seq", split_axis=0, concat_axis=1, tiled=True)
    y_rows = to_rows(y_back, chans)
    dz_rows = to_rows(dz_back, chans)
    y_f = y_rows.astype(jnp.float32)
    mixed = (sig_f + y_f * swish).astype(jnp.bfloat16)
    dz_flat = dz_rows.reshape(rows_here * chans, width_two)
    back = jnp.dot(dz_flat, right_eff, preferred_element_type=jnp.float32).reshape(
        rows_here, chans, width_two
    )
    dswish = gate * (1.0 + sig_f * (1.0 - gate))
    grad_signal = (cot_f * (1.0 + y_f * dswish) + back).astype(jnp.bfloat16)
    wide = z_cols.shape[2]
    z_flat = z_cols.reshape(width_one, wide)
    dy_flat = dy_cols.reshape(width_one, wide)
    left_term = lax.dot_general(
        dy_flat, z_flat, (((1,), (1,)), ((), ())), preferred_element_type=jnp.float32
    )
    right_term = lax.dot_general(
        dz_flat, flat_signal, (((0,), (0,)), ((), ())), preferred_element_type=jnp.float32
    )
    total_chans = chans * lax.axis_size("ch")
    right_term = right_term * right_mask.astype(jnp.float32) / math.sqrt(width_one * total_chans)
    left_term = left_term * left_mask.astype(jnp.float32) / math.sqrt(width_two * total_chans)
    partial_value = (
        lax.psum_scatter(right_term, "seq", scatter_dimension=0, tiled=True),
        lax.psum_scatter(left_term, "seq", scatter_dimension=0, tiled=True),
    )
    grad_right, grad_left = (
        lax.psum_scatter(partial_value[0], "ch", scatter_dimension=1, tiled=True),
        lax.psum_scatter(partial_value[1], "ch", scatter_dimension=1, tiled=True),
    )
    return (mixed, grad_signal, grad_right, grad_left)


def mix_kernel(peers, groups, parts, chunks, scales, *refs):
    right_blocks, left_blocks, signal, cotangent, right_in, left_in, *refs = refs
    out_m, out_g, out_r, out_l, xh, ch, mt, gt, *refs = refs
    right, left, grad_r, grad_l, xbuf, cbuf, zbuf, dybuf, dzbuf, *refs = refs
    pairs, along, first_out, first_in, second_out, second_in, slab, facing, turned, *refs = refs
    in_send, in_recv, own_in_sem, out_send, out_recv, last_recv, stage_sem, *refs = refs
    pair_sems, along_sems, first_sems, second_sems, load_sem, first_sem, free_sem, line_sem, all_sem = refs
    me = lax.axis_index("seq")
    column = lax.axis_index("ch")
    rows = signal.shape[0]
    width = signal.shape[2]
    order = left.shape[0]
    tile = 256
    piece = rows // chunks
    last = parts - 1
    others = peers - 1
    spare = parts % 2

    def own_rows(who):
        return pl.ds(pl.multiple_of(who * rows, rows), rows)

    def some_rows(who, chunk):
        return pl.ds(pl.multiple_of(who * rows + chunk * piece, piece), piece)

    def remote(source, target, going, coming, who):
        return pltpu.make_async_remote_copy(
            src_ref=source,
            dst_ref=target,
            send_sem=going,
            recv_sem=coming,
            device_id=(who, column),
            device_id_type=pl.DeviceIdType.MESH,
        )

    def take_all(ref, sem):
        pltpu.make_async_copy(ref, ref, sem).wait()

    def each_peer(action):
        @pl.loop(1, peers)
        def _(step):
            action(lax.rem(me + step, peers))

    barrier = pltpu.get_barrier_semaphore()

    def load(part, kind, source):
        there = pl.ds(pl.multiple_of(part * peers, peers), peers)
        return pltpu.make_async_copy(source.at[:, there, :], slab, load_sem.at[kind])

    def first_load(chunk):
        here = pl.ds(chunk * piece, piece)
        return pltpu.make_async_copy(signal.at[here, pl.ds(0, peers), :], slab.at[here], first_sem.at[chunk])

    for chunk in range(chunks):
        first_load(chunk).start()

    def tell(sem, who, line):
        pl.semaphore_signal(sem, inc=1, device_id=(who, line), device_id_type=pl.DeviceIdType.MESH)

    def tell_line(sem):
        @pl.loop(1, groups)
        def _(step):
            tell(sem, me, lax.rem(column + step, groups))

    gate = me == 0
    greeted = others + (groups - 1) * ((others - me) // others)

    @pl.when(gate)
    def _():
        tell_line(barrier)

    each_peer(lambda who: tell(barrier, who, column))

    inputs = ((0, signal, xh), (1, cotangent, ch))
    outputs = ((2, mt, xh, xbuf, out_m), (3, gt, ch, cbuf, out_g))

    def turn(part, kind, chunk, count):
        @pl.loop(chunk * (piece // 16), (chunk + count) * (piece // 16))
        def _(step):
            here = pl.ds(pl.multiple_of(step * 16, 16), 16)
            turned[lax.rem(part, 2), kind, :, here, :] = jnp.swapaxes(slab[here], 0, 1)

    def in_copy(kind, part, held, who, at_rows, there):
        return remote(
            turned.at[lax.rem(part, 2), kind, who, at_rows],
            held.at[part, there],
            in_send.at[kind, lax.rem(part, 2)],
            in_recv.at[kind, part],
            who,
        )

    def whole_in_copy(kind, part, held, who):
        return in_copy(kind, part, held, who, pl.ds(0, rows), own_rows(me))

    def own_copy(kind, part, held):
        return pltpu.make_async_copy(
            turned.at[lax.rem(part, 2), kind, me], held.at[part, own_rows(me)], own_in_sem.at[kind, lax.rem(part, 2)]
        )

    def send_in(part):
        for kind, source, held in inputs:
            load(part, kind, source).wait()
            turn(part, kind, 0, chunks)
            if kind == 0:
                load(part, 1, cotangent).start()
            each_peer(lambda who: whole_in_copy(kind, part, held, who).start())
            own_copy(kind, part, held).start()

    def send_first():
        for kind, source, held in inputs:
            if kind == 1:
                load(0, kind, source).wait()
            for chunk in range(chunks):
                if kind == 0:
                    first_load(chunk).wait()
                turn(0, kind, chunk, 1)
                if kind == 0 and chunk == 0:
                    pl.semaphore_wait(barrier, greeted)
                each_peer(
                    lambda who: in_copy(
                        kind, 0, held, who, pl.ds(chunk * piece, piece), some_rows(me, chunk)
                    ).start()
                )
            if kind == 0:
                load(0, 1, cotangent).start()
            own_copy(kind, 0, held).start()

    def wait_in(part):
        for kind, source, held in inputs:
            take_all(held.at[part, pl.ds(0, others * rows)], in_recv.at[kind, part])
            own_copy(kind, part, held).wait()

    def wait_in_sent(part):
        for kind, source, held in inputs:
            take_all(turned.at[lax.rem(part, 2), kind, pl.ds(0, others)], in_send.at[kind, lax.rem(part, 2)])

    def fetch(part):
        copies = [
            pltpu.make_async_copy(held.at[part], buf, stage_sem.at[kind - 2])
            for kind, landed, held, buf, out in outputs
        ]
        for copy in copies:
            copy.start()
        for copy in copies:
            copy.wait()

    def store(part):
        copies = []
        for kind, landed, held, buf, out in outputs:
            copies.append(pltpu.make_async_copy(buf, held.at[part], stage_sem.at[kind - 2]))
            copies.append(
                pltpu.make_async_copy(buf.at[own_rows(me)], landed.at[part * peers + me], stage_sem.at[kind])
            )
        for copy in copies:
            copy.start()
        for copy in copies:
            copy.wait()

    def send_out(part):
        def one(who):
            for kind, landed, held, buf, out in outputs:
                remote(
                    held.at[part, own_rows(who)], landed.at[part * peers + me],
                    out_send.at[kind - 2], out_recv.at[kind - 2, part], who,
                ).start()

        each_peer(one)

    def send_last(which):
        for chunk in which:
            for kind, landed, held, buf, out in outputs:
                each_peer(
                    lambda who: remote(
                        held.at[last, some_rows(who, chunk)],
                        turned.at[spare, kind - 2, me, pl.ds(chunk * piece, piece)],
                        out_send.at[kind - 2], last_recv.at[kind - 2, chunk], who,
                    ).start()
                )

    def turn_out(part):
        for kind, landed, held, buf, out in outputs:
            take_all(landed.at[pl.ds(part * peers, others)], out_recv.at[kind - 2, part])
            copy = pltpu.make_async_copy(landed.at[pl.ds(part * peers, peers)], facing, stage_sem.at[0])
            copy.start()
            copy.wait()

            @pl.loop(0, rows // 16)
            def _(step):
                here = pl.ds(pl.multiple_of(step * 16, 16), 16)
                out[here, part * peers:(part + 1) * peers, :] = jnp.swapaxes(facing[:, here, :], 0, 1)

    def keep_own():
        for kind, landed, held, buf, out in outputs:
            turned[spare, kind - 2, me] = buf[own_rows(me), :]

    def turn_last(which):
        for chunk in which:
            for kind, landed, held, buf, out in outputs:
                take_all(
                    turned.at[spare, kind - 2, pl.ds(0, others), pl.ds(chunk * piece, piece)],
                    last_recv.at[kind - 2, chunk],
                )

                @pl.loop(chunk * (piece // 16), (chunk + 1) * (piece // 16))
                def _(step):
                    here = pl.ds(pl.multiple_of(step * 16, 16), 16)
                    out[here, last * peers:parts * peers, :] = jnp.swapaxes(
                        turned[spare, kind - 2, :, here, :], 0, 1
                    )

    def wait_out_sent():
        for kind, landed, held, buf, out in outputs:
            take_all(held.at[:, pl.ds(0, others * rows)], out_send.at[kind - 2])

    def at(step):
        return pl.ds(pl.multiple_of(step * tile, tile), tile)

    def dot(a, b, dims):
        return lax.dot_general(a, b, (dims, ((), ())), preferred_element_type=jnp.float32)

    def compute():
        @pl.loop(0, order // tile)
        def _(step):
            x = xbuf[at(step), :]
            zbuf[at(step), :] = dot(x, right[...], ((1,), (1,))).astype(jnp.bfloat16)
            sig = x.astype(jnp.float32)
            swish = sig * jax.nn.sigmoid(sig)
            cot = cbuf[at(step), :].astype(jnp.float32)
            dybuf[at(step), :] = (cot * swish).astype(jnp.bfloat16)

        @pl.loop(0, order // tile)
        def _(step):
            dzbuf[at(step), :] = dot(left[:, at(step)], dybuf[...], ((0,), (0,))).astype(jnp.bfloat16)
            grad_l[at(step), :] += dot(dybuf[at(step), :], zbuf[...], ((1,), (1,)))

        @pl.loop(0, width // tile)
        def _(step):
            grad_r[at(step), :] += dot(dzbuf[:, at(step)], xbuf[...], ((0,), (0,)))

        @pl.loop(0, order // tile)
        def _(step):
            y = dot(left[at(step), :], zbuf[...], ((1,), (0,))).astype(jnp.bfloat16).astype(jnp.float32)
            back = dot(dzbuf[at(step), :], right[...], ((1,), (0,)))
            sig = xbuf[at(step), :].astype(jnp.float32)
            cot = cbuf[at(step), :].astype(jnp.float32)
            gate = jax.nn.sigmoid(sig)
            xbuf[at(step), :] = (sig + y * (sig * gate)).astype(jnp.bfloat16)
            dswish = gate * (1.0 + sig * (1.0 - gate))
            cbuf[at(step), :] = (cot * (1.0 + y * dswish) + back).astype(jnp.bfloat16)

    def apply_mask(blocks, target):
        side = target.shape[0] // blocks.shape[0]

        @pl.loop(0, blocks.shape[0])
        def _(down):
            here = pl.ds(pl.multiple_of(down * side, side), side)
            for right_of in range(blocks.shape[1]):
                there = slice(right_of * side, (right_of + 1) * side)
                keep = blocks[down, right_of].astype(jnp.float32)
                target[here, there] = (target[here, there].astype(jnp.float32) * keep).astype(jnp.bfloat16)

    half = peers // 2
    parity = lax.rem(me, 2)
    chip = me // 2
    sibling = me + 1 - 2 * parity
    cols = width // groups
    grads = ((0, grad_r, right_blocks), (1, grad_l, left_blocks))
    bits = ((1, 2), (2, 1))

    def own_cols(line):
        return pl.ds(pl.multiple_of(line * cols, cols), cols)

    def start_pairs():
        @pl.loop(0, half)
        def _(block):
            for kind, grad, blocks in grads:
                remote(
                    grad.at[own_rows(2 * block + 1 - parity)], pairs.at[kind, block],
                    pair_sems.at[0, kind], pair_sems.at[1, kind], sibling,
                ).start()

    def send_along():
        for kind, grad, blocks in grads:
            take_all(pairs.at[kind], pair_sems.at[1, kind])

            @pl.loop(0, half)
            def _(block):
                total = grad[own_rows(2 * block + parity), :] + pairs[kind, block]
                grad[own_rows(2 * block + parity), :] = total
                zbuf[own_rows(kind * half + block), :] = total.astype(jnp.bfloat16)

            @pl.loop(1, groups)
            def _(step):
                other = lax.rem(column + step, groups)
                pltpu.make_async_remote_copy(
                    src_ref=zbuf.at[pl.ds(kind * half * rows, half * rows), own_cols(other)],
                    dst_ref=along.at[kind, column],
                    send_sem=along_sems.at[0, kind],
                    recv_sem=along_sems.at[1, kind],
                    device_id=(me, other),
                    device_id_type=pl.DeviceIdType.MESH,
                ).start()

    def partner(step):
        who = chip
        for bit in (1, 2):
            if step & bit:
                who = who + bit * (1 - 2 * lax.rem(chip // bit, 2))
        return who

    def first_copy(kind):
        return remote(
            first_out.at[kind], first_in.at[kind], first_sems.at[0, kind], first_sems.at[1, kind],
            2 * partner(bits[kind][0]) + parity,
        )

    def second_copy(kind):
        return remote(
            second_out.at[kind], second_in.at[kind], second_sems.at[0, kind], second_sems.at[1, kind],
            2 * partner(bits[kind][1]) + parity,
        )

    def term(grad, block):
        return grad[own_rows(2 * block + parity), own_cols(column)]

    def sum_along():
        for kind, grad, blocks in grads:
            take_all(along.at[kind, pl.ds(0, groups - 1)], along_sems.at[1, kind])
            side = width // blocks.shape[0]

            @pl.loop(0, half)
            def _(block):
                whose = 2 * block + parity
                parts_of = []
                total = grad[own_rows(whose), own_cols(column)]
                for step in range(1, groups):
                    other = lax.rem(column + step, groups)
                    total = total + along[kind, other, own_rows(block), :].astype(jnp.float32)
                for right_of in range(cols // side):
                    there = slice(right_of * side, (right_of + 1) * side)
                    keep = blocks[whose * rows // side, column * (cols // side) + right_of].astype(jnp.float32)
                    parts_of.append(total[:, there] * keep / scales[kind])
                grad[own_rows(whose), own_cols(column)] = jnp.concatenate(parts_of, axis=1)

            for place, step in enumerate((bits[kind][0], 3)):
                first_out[kind, place] = term(grad, partner(step)).astype(jnp.bfloat16)
            first_copy(kind).start()

    def send_second():
        for kind, grad, blocks in grads:
            first_copy(kind).wait_recv()
            total = term(grad, partner(bits[kind][1])) + first_in[kind, 1].astype(jnp.float32)
            second_out[kind] = total.astype(jnp.bfloat16)
            second_copy(kind).start()

    def finish_sums():
        for (kind, grad, blocks), out in zip(grads, (out_r, out_l)):
            second_copy(kind).wait_recv()
            out[...] = (
                term(grad, chip) + first_in[kind, 0].astype(jnp.float32) + second_in[kind].astype(jnp.float32)
            )

    def wait_sums():
        for kind, grad, blocks in grads:
            take_all(pairs.at[kind], pair_sems.at[0, kind])
            take_all(along.at[kind, pl.ds(0, groups - 1)], along_sems.at[0, kind])
            first_copy(kind).wait_send()
            second_copy(kind).wait_send()

    fetched = (
        pltpu.make_async_copy(right_in, right, load_sem.at[2]),
        pltpu.make_async_copy(left_in, left, load_sem.at[3]),
    )
    send_first()
    if parts > 1:
        load(1, 0, signal).start()
    for copy in fetched:
        copy.start()

    @pl.when(gate)
    def _():
        tell_line(line_sem)

    if parts > 1:
        send_in(1)
    if parts > 2:
        load(2, 0, signal).start()
    for copy in fetched:
        copy.wait()
    grad_r[...] = jnp.zeros_like(grad_r)
    grad_l[...] = jnp.zeros_like(grad_l)
    apply_mask(right_blocks, right)
    apply_mask(left_blocks, left)

    @pl.when(gate)
    def _():
        pl.semaphore_wait(line_sem, groups - 1)
        each_peer(lambda who: tell(all_sem, who, column))

    @pl.loop(0, parts)
    def _(part):
        wait_in(part)

        @pl.when(part + 2 < parts)
        def _():
            wait_in_sent(part)
            send_in(part + 2)

        @pl.when(part + 3 < parts)
        def _():
            load(part + 3, 0, signal).start()

        @pl.when(part == last)
        def _():
            if parts > 1:
                wait_in_sent(last - 1)
            each_peer(lambda who: tell(free_sem, who, column))

        @pl.when(part >= 1)
        def _():
            send_out(part - 1)

        fetch(part)
        compute()

        @pl.when(part == last)
        def _():
            start_pairs()

        store(part)

    pl.semaphore_wait(free_sem, others)
    keep_own()

    @pl.when(me > 0)
    def _():
        pl.semaphore_wait(all_sem, 1)

    send_along()
    if last > 0:
        turn_out(0)
    sum_along()
    send_last(range(chunks // 2))
    for part in range(1, last):
        turn_out(part)
    send_second()
    send_last(range(chunks // 2, chunks))
    wait_in_sent(last)
    wait_sums()
    turn_last(range(chunks // 2))
    finish_sums()
    turn_last(range(chunks // 2, chunks))
    wait_out_sent()

def hand_over(*refs):
    sems, count = refs[-1], len(refs) // 2
    copies = [pltpu.make_async_copy(refs[at], refs[count + at], sems.at[at]) for at in range(count)]
    for copy in copies:
        copy.start()
    for copy in copies:
        copy.wait()


def shards_by_channel(signal, cotangent, right_factor, left_factor, right_blocks, left_blocks):
    rows_here, chans, width_two = signal.shape
    width_one = left_factor.shape[0]
    peers = lax.axis_size("seq")
    groups = lax.axis_size("ch")
    parts = chans // peers
    half = peers // 2
    cols = width_two // groups
    chunks = 4
    square = (width_one, width_two)
    scales = (math.sqrt(width_one * chans * groups), math.sqrt(width_two * chans * groups))
    hbm = pl.BlockSpec(memory_space=pl.ANY)
    vmem = pl.BlockSpec(memory_space=pltpu.VMEM)
    smem = pl.BlockSpec(memory_space=pltpu.SMEM)
    held = jax.ShapeDtypeStruct((parts, *square), jnp.bfloat16)
    landed = jax.ShapeDtypeStruct((chans, rows_here, width_two), jnp.bfloat16)
    results = ((signal.shape, jnp.bfloat16),) * 2 + (((rows_here, cols), jnp.float32),) * 2
    made = pl.pallas_call(
        functools.partial(mix_kernel, peers, groups, parts, chunks, scales),
        out_shape=tuple(pltpu.VMEM(*each) for each in results) + (held, held, landed, landed),
        in_specs=[smem, smem, hbm, hbm, hbm, hbm],
        out_specs=(vmem,) * 4 + (hbm,) * 4,
        scratch_shapes=[
            pltpu.VMEM(square, jnp.bfloat16),
            pltpu.VMEM(square, jnp.bfloat16),
            pltpu.VMEM(square, jnp.float32),
            pltpu.VMEM(square, jnp.float32),
            pltpu.VMEM(square, jnp.bfloat16),
            pltpu.VMEM(square, jnp.bfloat16),
            pltpu.VMEM(square, jnp.bfloat16),
            pltpu.VMEM(square, jnp.bfloat16),
            pltpu.VMEM(square, jnp.bfloat16),
            pltpu.VMEM((2, half, rows_here, width_two), jnp.float32),
            pltpu.VMEM((2, groups, half * rows_here, cols), jnp.bfloat16),
            pltpu.VMEM((2, 2, rows_here, cols), jnp.bfloat16),
            pltpu.VMEM((2, 2, rows_here, cols), jnp.bfloat16),
            pltpu.VMEM((2, rows_here, cols), jnp.bfloat16),
            pltpu.VMEM((2, rows_here, cols), jnp.bfloat16),
            pltpu.VMEM((rows_here, peers, width_two), jnp.bfloat16),
            pltpu.VMEM((peers, rows_here, width_two), jnp.bfloat16),
            pltpu.VMEM((2, 2, peers, rows_here, width_two), jnp.bfloat16),
            pltpu.SemaphoreType.DMA((2, 2)),
            pltpu.SemaphoreType.DMA((2, parts)),
            pltpu.SemaphoreType.DMA((2, 2)),
            pltpu.SemaphoreType.DMA((2,)),
            pltpu.SemaphoreType.DMA((2, parts)),
            pltpu.SemaphoreType.DMA((2, chunks)),
            pltpu.SemaphoreType.DMA((4,)),
            pltpu.SemaphoreType.DMA((2, 2)),
            pltpu.SemaphoreType.DMA((2, 2)),
            pltpu.SemaphoreType.DMA((2, 2)),
            pltpu.SemaphoreType.DMA((2, 2)),
            pltpu.SemaphoreType.DMA((4,)),
            pltpu.SemaphoreType.DMA((chunks,)),
            pltpu.SemaphoreType.REGULAR,
            pltpu.SemaphoreType.REGULAR,
            pltpu.SemaphoreType.REGULAR,
        ],
        compiler_params=pltpu.CompilerParams(
            collective_id=0, has_side_effects=True, vmem_limit_bytes=47 * 2**20
        ),
    )(right_blocks, left_blocks, signal, cotangent, right_factor, left_factor)
    made = [pltpu.with_memory_space_constraint(array, pltpu.VMEM) for array in made[:4]]
    return pl.pallas_call(
        hand_over,
        out_shape=tuple(jax.ShapeDtypeStruct(*each) for each in results),
        in_specs=[vmem] * 4,
        out_specs=(hbm,) * 4,
        scratch_shapes=[pltpu.SemaphoreType.DMA((4,))],
        compiler_params=pltpu.CompilerParams(vmem_limit_bytes=2**20),
    )(*made)


def shards(signal, *others):
    rows_here, chans, width_two = signal.shape
    peers = lax.axis_size("seq")
    width_one = others[1].shape[0]
    sides = (width_two // others[3].shape[0], width_one // others[4].shape[0])
    fits = chans % peers == 0 and rows_here % 16 == 0 and peers == 8
    fits = fits and sides == (128, 128) and rows_here == 128
    fits = fits and width_two // lax.axis_size("ch") % 128 == 0
    if fits and width_one == 1024 and width_two == 1024 and chans // peers <= 4:
        return shards_by_channel(signal, *others)
    return shards_by_column(signal, *others)


def solution(mesh):
    return jax.shard_map(
        shards,
        mesh=mesh,
        in_specs=(P("seq", "ch", None), P("seq", "ch", None), P(), P(), P(), P()),
        out_specs=(P("seq", "ch", None), P("seq", "ch", None), P("seq", "ch"), P("seq", "ch")),
        check_vma=False,
    )
```

```python
import functools
import math

import jax
import jax.numpy as jnp
from jax import lax
from jax.experimental import pallas as pl
from jax.experimental.pallas import tpu as pltpu
from jax.sharding import PartitionSpec as P


def expand(blocks, width):
    tile = width // blocks.shape[0]
    return jnp.repeat(jnp.repeat(blocks, tile, axis=0), tile, axis=1)


def to_columns(rows, peers):
    rows_here, chans, width_two = rows.shape
    piece = width_two // peers
    arranged = rows.reshape(rows_here, chans, peers, piece).transpose(0, 2, 1, 3)
    return arranged.reshape(rows_here, peers, chans * piece)


def to_rows(received, chans):
    rows_here, peers, wide = received.shape
    piece = wide // chans
    arranged = received.reshape(rows_here, peers, chans, piece).transpose(0, 2, 1, 3)
    return arranged.reshape(rows_here, chans, peers * piece)


def shards_by_column(signal, cotangent, right_factor, left_factor, right_blocks, left_blocks):
    rows_here, chans, width_two = signal.shape
    width_one = left_factor.shape[0]
    peers = lax.axis_size("seq")
    right_mask = expand(right_blocks, width_two).astype(jnp.bfloat16)
    left_mask = expand(left_blocks, width_one).astype(jnp.bfloat16)
    right_eff = right_factor * right_mask
    left_eff = left_factor * left_mask
    flat_signal = signal.reshape(rows_here * chans, width_two)
    first_rows = jnp.dot(flat_signal, right_eff.T, preferred_element_type=jnp.float32)
    first_rows = to_columns(
        first_rows.astype(jnp.bfloat16).reshape(rows_here, chans, width_two), peers
    )
    sig_f = signal.astype(jnp.float32)
    gate = jax.nn.sigmoid(sig_f)
    swish = sig_f * gate
    cot_f = cotangent.astype(jnp.float32)
    grad_rows = to_columns((cot_f * swish).astype(jnp.bfloat16), peers)
    z_cols = lax.all_to_all(first_rows, "seq", split_axis=1, concat_axis=0, tiled=True)
    flat_cols = z_cols.reshape(width_one, z_cols.shape[2])
    result = jnp.dot(left_eff, flat_cols, preferred_element_type=jnp.float32)
    y_cols = result.astype(jnp.bfloat16).reshape(width_one, 1, z_cols.shape[2])
    y_back = lax.all_to_all(y_cols, "seq", split_axis=0, concat_axis=1, tiled=True)
    dy_cols = lax.all_to_all(grad_rows, "seq", split_axis=1, concat_axis=0, tiled=True)
    flat_cols = dy_cols.reshape(width_one, dy_cols.shape[2])
    result = lax.dot_general(
        left_eff, flat_cols, (((0,), (0,)), ((), ())), preferred_element_type=jnp.float32
    )
    dz_cols = result.astype(jnp.bfloat16).reshape(width_one, 1, dy_cols.shape[2])
    dz_back = lax.all_to_all(dz_cols, "seq", split_axis=0, concat_axis=1, tiled=True)
    y_rows = to_rows(y_back, chans)
    dz_rows = to_rows(dz_back, chans)
    y_f = y_rows.astype(jnp.float32)
    mixed = (sig_f + y_f * swish).astype(jnp.bfloat16)
    dz_flat = dz_rows.reshape(rows_here * chans, width_two)
    back = jnp.dot(dz_flat, right_eff, preferred_element_type=jnp.float32).reshape(
        rows_here, chans, width_two
    )
    dswish = gate * (1.0 + sig_f * (1.0 - gate))
    grad_signal = (cot_f * (1.0 + y_f * dswish) + back).astype(jnp.bfloat16)
    wide = z_cols.shape[2]
    z_flat = z_cols.reshape(width_one, wide)
    dy_flat = dy_cols.reshape(width_one, wide)
    left_term = lax.dot_general(
        dy_flat, z_flat, (((1,), (1,)), ((), ())), preferred_element_type=jnp.float32
    )
    right_term = lax.dot_general(
        dz_flat, flat_signal, (((0,), (0,)), ((), ())), preferred_element_type=jnp.float32
    )
    total_chans = chans * lax.axis_size("ch")
    right_term = right_term * right_mask.astype(jnp.float32) / math.sqrt(width_one * total_chans)
    left_term = left_term * left_mask.astype(jnp.float32) / math.sqrt(width_two * total_chans)
    partial_value = (
        lax.psum_scatter(right_term, "seq", scatter_dimension=0, tiled=True),
        lax.psum_scatter(left_term, "seq", scatter_dimension=0, tiled=True),
    )
    grad_right, grad_left = (
        lax.psum_scatter(partial_value[0], "ch", scatter_dimension=1, tiled=True),
        lax.psum_scatter(partial_value[1], "ch", scatter_dimension=1, tiled=True),
    )
    return (mixed, grad_signal, grad_right, grad_left)


def mix_kernel(peers, groups, parts, chunks, scales, *refs):
    right_blocks, left_blocks, signal, cotangent, right_in, left_in, *refs = refs
    out_m, out_g, out_r, out_l, xh, ch, mt, gt, *refs = refs
    right, left, grad_r, grad_l, xbuf, cbuf, zbuf, dybuf, dzbuf, *refs = refs
    pairs, along, first_out, first_in, second_out, second_in, slab, facing, turned, *refs = refs
    in_send, in_recv, own_in_sem, out_send, out_recv, last_recv, stage_sem, *refs = refs
    pair_sems, along_sems, first_sems, second_sems, load_sem, first_sem, free_sem, line_sem, all_sem = refs
    me = lax.axis_index("seq")
    column = lax.axis_index("ch")
    rows = signal.shape[0]
    width = signal.shape[2]
    order = left.shape[0]
    tile = 256
    piece = rows // chunks
    last = parts - 1
    others = peers - 1
    spare = parts % 2

    def own_rows(who):
        return pl.ds(pl.multiple_of(who * rows, rows), rows)

    def some_rows(who, chunk):
        return pl.ds(pl.multiple_of(who * rows + chunk * piece, piece), piece)

    def remote(source, target, going, coming, who):
        return pltpu.make_async_remote_copy(
            src_ref=source,
            dst_ref=target,
            send_sem=going,
            recv_sem=coming,
            device_id=(who, column),
            device_id_type=pl.DeviceIdType.MESH,
        )

    def take_all(ref, sem):
        pltpu.make_async_copy(ref, ref, sem).wait()

    def each_peer(action):
        @pl.loop(1, peers)
        def _(step):
            action(lax.rem(me + step, peers))

    barrier = pltpu.get_barrier_semaphore()

    def load(part, kind, source):
        there = pl.ds(pl.multiple_of(part * peers, peers), peers)
        return pltpu.make_async_copy(source.at[:, there, :], slab, load_sem.at[kind])

    def first_load(chunk):
        here = pl.ds(chunk * piece, piece)
        return pltpu.make_async_copy(signal.at[here, pl.ds(0, peers), :], slab.at[here], first_sem.at[chunk])

    for chunk in range(chunks):
        first_load(chunk).start()

    def tell(sem, who, line):
        pl.semaphore_signal(sem, inc=1, device_id=(who, line), device_id_type=pl.DeviceIdType.MESH)

    def tell_line(sem):
        @pl.loop(1, groups)
        def _(step):
            tell(sem, me, lax.rem(column + step, groups))

    gate = me == others
    greeted = others + (groups - 1) * (me // others)

    @pl.when(gate)
    def _():
        tell_line(barrier)

    each_peer(lambda who: tell(barrier, who, column))

    inputs = ((0, signal, xh), (1, cotangent, ch))
    outputs = ((2, mt, xh, xbuf, out_m), (3, gt, ch, cbuf, out_g))

    def turn(part, kind, chunk, count):
        @pl.loop(chunk * (piece // 16), (chunk + count) * (piece // 16))
        def _(step):
            here = pl.ds(pl.multiple_of(step * 16, 16), 16)
            turned[lax.rem(part, 2), kind, :, here, :] = jnp.swapaxes(slab[here], 0, 1)

    def in_copy(kind, part, held, who, at_rows, there):
        return remote(
            turned.at[lax.rem(part, 2), kind, who, at_rows],
            held.at[part, there],
            in_send.at[kind, lax.rem(part, 2)],
            in_recv.at[kind, part],
            who,
        )

    def whole_in_copy(kind, part, held, who):
        return in_copy(kind, part, held, who, pl.ds(0, rows), own_rows(me))

    def own_copy(kind, part, held):
        return pltpu.make_async_copy(
            turned.at[lax.rem(part, 2), kind, me], held.at[part, own_rows(me)], own_in_sem.at[kind, lax.rem(part, 2)]
        )

    def send_in(part):
        for kind, source, held in inputs:
            load(part, kind, source).wait()
            turn(part, kind, 0, chunks)
            if kind == 0:
                load(part, 1, cotangent).start()
            each_peer(lambda who: whole_in_copy(kind, part, held, who).start())
            own_copy(kind, part, held).start()

    def send_first():
        for kind, source, held in inputs:
            if kind == 1:
                load(0, kind, source).wait()
            for chunk in range(chunks):
                if kind == 0:
                    first_load(chunk).wait()
                turn(0, kind, chunk, 1)
                if kind == 0 and chunk == 0:
                    pl.semaphore_wait(barrier, greeted)
                each_peer(
                    lambda who: in_copy(
                        kind, 0, held, who, pl.ds(chunk * piece, piece), some_rows(me, chunk)
                    ).start()
                )
            if kind == 0:
                load(0, 1, cotangent).start()
            own_copy(kind, 0, held).start()

    def wait_in(part):
        for kind, source, held in inputs:
            take_all(held.at[part, pl.ds(0, others * rows)], in_recv.at[kind, part])
            own_copy(kind, part, held).wait()

    def wait_in_sent(part):
        for kind, source, held in inputs:
            take_all(turned.at[lax.rem(part, 2), kind, pl.ds(0, others)], in_send.at[kind, lax.rem(part, 2)])

    def fetch(part):
        copies = [
            pltpu.make_async_copy(held.at[part], buf, stage_sem.at[kind - 2])
            for kind, landed, held, buf, out in outputs
        ]
        for copy in copies:
            copy.start()
        for copy in copies:
            copy.wait()

    def store(part):
        copies = []
        for kind, landed, held, buf, out in outputs:
            copies.append(pltpu.make_async_copy(buf, held.at[part], stage_sem.at[kind - 2]))
            copies.append(
                pltpu.make_async_copy(buf.at[own_rows(me)], landed.at[part * peers + me], stage_sem.at[kind])
            )
        for copy in copies:
            copy.start()
        for copy in copies:
            copy.wait()

    def send_out(part):
        def one(who):
            for kind, landed, held, buf, out in outputs:
                remote(
                    held.at[part, own_rows(who)], landed.at[part * peers + me],
                    out_send.at[kind - 2], out_recv.at[kind - 2, part], who,
                ).start()

        each_peer(one)

    def send_last(which):
        for chunk in which:
            for kind, landed, held, buf, out in outputs:
                each_peer(
                    lambda who: remote(
                        held.at[last, some_rows(who, chunk)],
                        turned.at[spare, kind - 2, me, pl.ds(chunk * piece, piece)],
                        out_send.at[kind - 2], last_recv.at[kind - 2, chunk], who,
                    ).start()
                )

    def turn_out(part):
        for kind, landed, held, buf, out in outputs:
            take_all(landed.at[pl.ds(part * peers, others)], out_recv.at[kind - 2, part])
            copy = pltpu.make_async_copy(landed.at[pl.ds(part * peers, peers)], facing, stage_sem.at[0])
            copy.start()
            copy.wait()

            @pl.loop(0, rows // 16)
            def _(step):
                here = pl.ds(pl.multiple_of(step * 16, 16), 16)
                out[here, part * peers:(part + 1) * peers, :] = jnp.swapaxes(facing[:, here, :], 0, 1)

    def keep_own():
        for kind, landed, held, buf, out in outputs:
            turned[spare, kind - 2, me] = buf[own_rows(me), :]

    def turn_last(which):
        for chunk in which:
            for kind, landed, held, buf, out in outputs:
                take_all(
                    turned.at[spare, kind - 2, pl.ds(0, others), pl.ds(chunk * piece, piece)],
                    last_recv.at[kind - 2, chunk],
                )

                @pl.loop(chunk * (piece // 16), (chunk + 1) * (piece // 16))
                def _(step):
                    here = pl.ds(pl.multiple_of(step * 16, 16), 16)
                    out[here, last * peers:parts * peers, :] = jnp.swapaxes(
                        turned[spare, kind - 2, :, here, :], 0, 1
                    )

    def wait_out_sent():
        for kind, landed, held, buf, out in outputs:
            take_all(held.at[:, pl.ds(0, others * rows)], out_send.at[kind - 2])

    def at(step):
        return pl.ds(pl.multiple_of(step * tile, tile), tile)

    def dot(a, b, dims):
        return lax.dot_general(a, b, (dims, ((), ())), preferred_element_type=jnp.float32)

    def compute():
        @pl.loop(0, order // tile)
        def _(step):
            x = xbuf[at(step), :]
            zbuf[at(step), :] = dot(x, right[...], ((1,), (1,))).astype(jnp.bfloat16)
            sig = x.astype(jnp.float32)
            swish = sig * jax.nn.sigmoid(sig)
            cot = cbuf[at(step), :].astype(jnp.float32)
            dybuf[at(step), :] = (cot * swish).astype(jnp.bfloat16)

        @pl.loop(0, order // tile)
        def _(step):
            dzbuf[at(step), :] = dot(left[:, at(step)], dybuf[...], ((0,), (0,))).astype(jnp.bfloat16)
            grad_l[at(step), :] += dot(dybuf[at(step), :], zbuf[...], ((1,), (1,)))

        @pl.loop(0, width // tile)
        def _(step):
            grad_r[at(step), :] += dot(dzbuf[:, at(step)], xbuf[...], ((0,), (0,)))

        @pl.loop(0, order // tile)
        def _(step):
            y = dot(left[at(step), :], zbuf[...], ((1,), (0,))).astype(jnp.bfloat16).astype(jnp.float32)
            back = dot(dzbuf[at(step), :], right[...], ((1,), (0,)))
            sig = xbuf[at(step), :].astype(jnp.float32)
            cot = cbuf[at(step), :].astype(jnp.float32)
            gate = jax.nn.sigmoid(sig)
            xbuf[at(step), :] = (sig + y * (sig * gate)).astype(jnp.bfloat16)
            dswish = gate * (1.0 + sig * (1.0 - gate))
            cbuf[at(step), :] = (cot * (1.0 + y * dswish) + back).astype(jnp.bfloat16)

    def apply_mask(blocks, target):
        side = target.shape[0] // blocks.shape[0]

        @pl.loop(0, blocks.shape[0])
        def _(down):
            here = pl.ds(pl.multiple_of(down * side, side), side)
            for right_of in range(blocks.shape[1]):
                there = slice(right_of * side, (right_of + 1) * side)
                keep = blocks[down, right_of].astype(jnp.float32)
                target[here, there] = (target[here, there].astype(jnp.float32) * keep).astype(jnp.bfloat16)

    half = peers // 2
    parity = lax.rem(me, 2)
    chip = me // 2
    sibling = me + 1 - 2 * parity
    cols = width // groups
    grads = ((0, grad_r, right_blocks), (1, grad_l, left_blocks))
    bits = ((1, 2), (2, 1))

    def own_cols(line):
        return pl.ds(pl.multiple_of(line * cols, cols), cols)

    def start_pairs():
        @pl.loop(0, half)
        def _(block):
            for kind, grad, blocks in grads:
                remote(
                    grad.at[own_rows(2 * block + 1 - parity)], pairs.at[kind, block],
                    pair_sems.at[0, kind], pair_sems.at[1, kind], sibling,
                ).start()

    def send_along():
        for kind, grad, blocks in grads:
            take_all(pairs.at[kind], pair_sems.at[1, kind])

            @pl.loop(0, half)
            def _(block):
                total = grad[own_rows(2 * block + parity), :] + pairs[kind, block]
                grad[own_rows(2 * block + parity), :] = total
                zbuf[own_rows(kind * half + block), :] = total.astype(jnp.bfloat16)

            @pl.loop(1, groups)
            def _(step):
                other = lax.rem(column + step, groups)
                pltpu.make_async_remote_copy(
                    src_ref=zbuf.at[pl.ds(kind * half * rows, half * rows), own_cols(other)],
                    dst_ref=along.at[kind, column],
                    send_sem=along_sems.at[0, kind],
                    recv_sem=along_sems.at[1, kind],
                    device_id=(me, other),
                    device_id_type=pl.DeviceIdType.MESH,
                ).start()

    def partner(step):
        who = chip
        for bit in (1, 2):
            if step & bit:
                who = who + bit * (1 - 2 * lax.rem(chip // bit, 2))
        return who

    def first_copy(kind):
        return remote(
            first_out.at[kind], first_in.at[kind], first_sems.at[0, kind], first_sems.at[1, kind],
            2 * partner(bits[kind][0]) + parity,
        )

    def second_copy(kind):
        return remote(
            second_out.at[kind], second_in.at[kind], second_sems.at[0, kind], second_sems.at[1, kind],
            2 * partner(bits[kind][1]) + parity,
        )

    def term(grad, block):
        return grad[own_rows(2 * block + parity), own_cols(column)]

    def sum_along():
        for kind, grad, blocks in grads:
            take_all(along.at[kind, pl.ds(0, groups - 1)], along_sems.at[1, kind])
            side = width // blocks.shape[0]

            @pl.loop(0, half)
            def _(block):
                whose = 2 * block + parity
                parts_of = []
                total = grad[own_rows(whose), own_cols(column)]
                for step in range(1, groups):
                    other = lax.rem(column + step, groups)
                    total = total + along[kind, other, own_rows(block), :].astype(jnp.float32)
                for right_of in range(cols // side):
                    there = slice(right_of * side, (right_of + 1) * side)
                    keep = blocks[whose * rows // side, column * (cols // side) + right_of].astype(jnp.float32)
                    parts_of.append(total[:, there] * keep / scales[kind])
                grad[own_rows(whose), own_cols(column)] = jnp.concatenate(parts_of, axis=1)

            for place, step in enumerate((bits[kind][0], 3)):
                first_out[kind, place] = term(grad, partner(step)).astype(jnp.bfloat16)
            first_copy(kind).start()

    def send_second():
        for kind, grad, blocks in grads:
            first_copy(kind).wait_recv()
            total = term(grad, partner(bits[kind][1])) + first_in[kind, 1].astype(jnp.float32)
            second_out[kind] = total.astype(jnp.bfloat16)
            second_copy(kind).start()

    def finish_sums():
        for (kind, grad, blocks), out in zip(grads, (out_r, out_l)):
            second_copy(kind).wait_recv()
            out[...] = (
                term(grad, chip) + first_in[kind, 0].astype(jnp.float32) + second_in[kind].astype(jnp.float32)
            )

    def wait_sums():
        for kind, grad, blocks in grads:
            take_all(pairs.at[kind], pair_sems.at[0, kind])
            take_all(along.at[kind, pl.ds(0, groups - 1)], along_sems.at[0, kind])
            first_copy(kind).wait_send()
            second_copy(kind).wait_send()

    fetched = (
        pltpu.make_async_copy(right_in, right, load_sem.at[2]),
        pltpu.make_async_copy(left_in, left, load_sem.at[3]),
    )
    send_first()
    if parts > 1:
        load(1, 0, signal).start()
    for copy in fetched:
        copy.start()

    @pl.when(gate)
    def _():
        tell_line(line_sem)

    if parts > 1:
        send_in(1)
    if parts > 2:
        load(2, 0, signal).start()
    for copy in fetched:
        copy.wait()
    grad_r[...] = jnp.zeros_like(grad_r)
    grad_l[...] = jnp.zeros_like(grad_l)
    apply_mask(right_blocks, right)
    apply_mask(left_blocks, left)

    @pl.when(gate)
    def _():
        pl.semaphore_wait(line_sem, groups - 1)
        each_peer(lambda who: tell(all_sem, who, column))

    @pl.loop(0, parts)
    def _(part):
        wait_in(part)

        @pl.when(part + 2 < parts)
        def _():
            wait_in_sent(part)
            send_in(part + 2)

        @pl.when(part + 3 < parts)
        def _():
            load(part + 3, 0, signal).start()

        @pl.when(part == last)
        def _():
            if parts > 1:
                wait_in_sent(last - 1)
            each_peer(lambda who: tell(free_sem, who, column))

        @pl.when(part >= 1)
        def _():
            send_out(part - 1)

        fetch(part)
        compute()

        @pl.when(part == last)
        def _():
            start_pairs()

        store(part)

    pl.semaphore_wait(free_sem, others)
    keep_own()

    @pl.when(me < others)
    def _():
        pl.semaphore_wait(all_sem, 1)

    send_along()
    if last > 0:
        turn_out(0)
    sum_along()
    send_last(range(chunks // 2))
    for part in range(1, last):
        turn_out(part)
    send_second()
    send_last(range(chunks // 2, chunks))
    wait_in_sent(last)
    wait_sums()
    turn_last(range(chunks // 2))
    finish_sums()
    turn_last(range(chunks // 2, chunks))
    wait_out_sent()

def hand_over(*refs):
    sems, count = refs[-1], len(refs) // 2
    copies = [pltpu.make_async_copy(refs[at], refs[count + at], sems.at[at]) for at in range(count)]
    for copy in copies:
        copy.start()
    for copy in copies:
        copy.wait()


def shards_by_channel(signal, cotangent, right_factor, left_factor, right_blocks, left_blocks):
    rows_here, chans, width_two = signal.shape
    width_one = left_factor.shape[0]
    peers = lax.axis_size("seq")
    groups = lax.axis_size("ch")
    parts = chans // peers
    half = peers // 2
    cols = width_two // groups
    chunks = 4
    square = (width_one, width_two)
    scales = (math.sqrt(width_one * chans * groups), math.sqrt(width_two * chans * groups))
    hbm = pl.BlockSpec(memory_space=pl.ANY)
    vmem = pl.BlockSpec(memory_space=pltpu.VMEM)
    smem = pl.BlockSpec(memory_space=pltpu.SMEM)
    held = jax.ShapeDtypeStruct((parts, *square), jnp.bfloat16)
    landed = jax.ShapeDtypeStruct((chans, rows_here, width_two), jnp.bfloat16)
    results = ((signal.shape, jnp.bfloat16),) * 2 + (((rows_here, cols), jnp.float32),) * 2
    made = pl.pallas_call(
        functools.partial(mix_kernel, peers, groups, parts, chunks, scales),
        out_shape=tuple(pltpu.VMEM(*each) for each in results) + (held, held, landed, landed),
        in_specs=[smem, smem, hbm, hbm, hbm, hbm],
        out_specs=(vmem,) * 4 + (hbm,) * 4,
        scratch_shapes=[
            pltpu.VMEM(square, jnp.bfloat16),
            pltpu.VMEM(square, jnp.bfloat16),
            pltpu.VMEM(square, jnp.float32),
            pltpu.VMEM(square, jnp.float32),
            pltpu.VMEM(square, jnp.bfloat16),
            pltpu.VMEM(square, jnp.bfloat16),
            pltpu.VMEM(square, jnp.bfloat16),
            pltpu.VMEM(square, jnp.bfloat16),
            pltpu.VMEM(square, jnp.bfloat16),
            pltpu.VMEM((2, half, rows_here, width_two), jnp.float32),
            pltpu.VMEM((2, groups, half * rows_here, cols), jnp.bfloat16),
            pltpu.VMEM((2, 2, rows_here, cols), jnp.bfloat16),
            pltpu.VMEM((2, 2, rows_here, cols), jnp.bfloat16),
            pltpu.VMEM((2, rows_here, cols), jnp.bfloat16),
            pltpu.VMEM((2, rows_here, cols), jnp.bfloat16),
            pltpu.VMEM((rows_here, peers, width_two), jnp.bfloat16),
            pltpu.VMEM((peers, rows_here, width_two), jnp.bfloat16),
            pltpu.VMEM((2, 2, peers, rows_here, width_two), jnp.bfloat16),
            pltpu.SemaphoreType.DMA((2, 2)),
            pltpu.SemaphoreType.DMA((2, parts)),
            pltpu.SemaphoreType.DMA((2, 2)),
            pltpu.SemaphoreType.DMA((2,)),
            pltpu.SemaphoreType.DMA((2, parts)),
            pltpu.SemaphoreType.DMA((2, chunks)),
            pltpu.SemaphoreType.DMA((4,)),
            pltpu.SemaphoreType.DMA((2, 2)),
            pltpu.SemaphoreType.DMA((2, 2)),
            pltpu.SemaphoreType.DMA((2, 2)),
            pltpu.SemaphoreType.DMA((2, 2)),
            pltpu.SemaphoreType.DMA((4,)),
            pltpu.SemaphoreType.DMA((chunks,)),
            pltpu.SemaphoreType.REGULAR,
            pltpu.SemaphoreType.REGULAR,
            pltpu.SemaphoreType.REGULAR,
        ],
        compiler_params=pltpu.CompilerParams(
            collective_id=0, has_side_effects=True, vmem_limit_bytes=47 * 2**20
        ),
    )(right_blocks, left_blocks, signal, cotangent, right_factor, left_factor)
    made = [pltpu.with_memory_space_constraint(array, pltpu.VMEM) for array in made[:4]]
    return pl.pallas_call(
        hand_over,
        out_shape=tuple(jax.ShapeDtypeStruct(*each) for each in results),
        in_specs=[vmem] * 4,
        out_specs=(hbm,) * 4,
        scratch_shapes=[pltpu.SemaphoreType.DMA((4,))],
        compiler_params=pltpu.CompilerParams(vmem_limit_bytes=2**20),
    )(*made)


def shards(signal, *others):
    rows_here, chans, width_two = signal.shape
    peers = lax.axis_size("seq")
    width_one = others[1].shape[0]
    sides = (width_two // others[3].shape[0], width_one // others[4].shape[0])
    fits = chans % peers == 0 and rows_here % 16 == 0 and peers == 8
    fits = fits and sides == (128, 128) and rows_here == 128
    fits = fits and width_two // lax.axis_size("ch") % 128 == 0
    if fits and width_one == 1024 and width_two == 1024 and chans // peers <= 4:
        return shards_by_channel(signal, *others)
    return shards_by_column(signal, *others)


def solution(mesh):
    return jax.shard_map(
        shards,
        mesh=mesh,
        in_specs=(P("seq", "ch", None), P("seq", "ch", None), P(), P(), P(), P()),
        out_specs=(P("seq", "ch", None), P("seq", "ch", None), P("seq", "ch"), P("seq", "ch")),
        check_vma=False,
    )
```
